32 devices in a mesh: wide: 8 (over z, x), narrow: 4 (over y, core).
Axes of the slice: x: 2, y: 2, z: 4, core: 2. Of those that a mesh axis runs over, the one named last changes fastest.
Arguments:
- pair_act: bfloat16 [768, 768, 128], P('wide', 'narrow'), may hold values from -6 to 6
- residue_mask: int32 [768], replicated, may hold values 0 or 1
- w_proj_start: bfloat16 [128, 512], replicated, may hold values from -0.5 to 0.5
- w_bias_start: bfloat16 [128, 4], replicated, may hold values from -40 to 40
- w_out_start: bfloat16 [128, 128], replicated, may hold values from -0.5 to 0.5
- w_proj_end: bfloat16 [128, 512], replicated, may hold values from -0.5 to 0.5
- w_bias_end: bfloat16 [128, 4], replicated, may hold values from -40 to 40
- w_out_end: bfloat16 [128, 128], replicated, may hold values from -0.5 to 0.5
Outputs:
- update_start: bfloat16 [768, 768, 128], P('wide', 'narrow')
- update_end: bfloat16 [768, 768, 128], P('wide', 'narrow')
The draws below stay inside these ranges and needn't reach their ends.
All inputs are finite; a program needn't handle non-finite values.
Results may differ from the reference program's by a relative error of at most 0.012.
The reference program's roundings to bfloat16 on the way count: a program that leaves them out, or rounds other values in their place, can miss the bound.
Values may be sent and summed in bfloat16 or wider, within the bound.
No kernel may reach another device: no remote copies, remote signals or barrier semaphores. Data moves between devices by JAX's collectives and lax.ppermute only.
A program may use at most 128 MiB of HBM per device.

```python
import jax
import jax.numpy as jnp
from jax import lax

N = 768
C = 128
HEADS = 4
HEAD_DIM = 32


def bias_columns(key, salt):
    key = jax.random.fold_in(key, salt)
    first_key = jax.random.fold_in(key, 0)
    third_key = jax.random.fold_in(key, 2)
    base = jax.random.truncated_normal(first_key, -4.0, 4.0, (C, HEADS), jnp.float32) * 128.0 ** (-0.5)
    factors = jax.random.uniform(third_key, (HEADS,), jnp.float32, 0.5, 2.0)
    return (base * factors[None, :]).astype(jnp.bfloat16)


def draw_w_bias_start(key, part):
    return bias_columns(key, 1701)


def draw_w_bias_end(key, part):
    return bias_columns(key, 2903)


def plant(drawn, own_key, smallest, top_value):
    spot = [jax.random.randint(jax.random.fold_in(own_key, axis), (), 0, length) for axis, length in enumerate(drawn.shape)]
    widest = drawn.shape.index(max(drawn.shape))
    next_to = spot[:widest] + [(spot[widest] + 1) % drawn.shape[widest]] + spot[widest + 1:]
    return drawn.at[tuple(spot)].set(smallest).at[tuple(next_to)].set(top_value)


def shard_levels(own_key, extent, shards, low, high):
    level = 1.0
    for axis_at, parts in shards:
        heights = jax.random.uniform(jax.random.fold_in(jax.random.fold_in(own_key, 6), axis_at), (parts,), jnp.float32, low / len(shards), high / len(shards))
        level = level * jnp.repeat(jnp.exp(heights), extent[axis_at] // parts).reshape((-1,) + (1,) * (len(extent) - 1 - axis_at))
    return level


def bell_draw(key, extent, scale, reach, cuts=(), held_as=jnp.bfloat16):
    array = scale * jax.random.normal(key, extent, jnp.float32)
    if cuts:
        array = array * shard_levels(key, extent, cuts, -0.22, 0.18)
    return jnp.clip(array, -reach, reach).astype(held_as)


def setup_inputs(seed: int = 0) -> dict:
    arg_keys = jax.random.split(jax.random.key(seed), 9)
    return {
        "pair_act": bell_draw(arg_keys[0], (N, N, C), 1.0, 6.0, ((0, 8), (1, 4))),
        "residue_mask": plant((jax.random.randint(arg_keys[1], (N,), 0, 8) < 7).astype(jnp.int32), jax.random.fold_in(arg_keys[1], 1), 0, 1),
        "w_proj_start": bell_draw(arg_keys[2], (C, HEADS * 4 * HEAD_DIM), C ** -0.5, 0.5),
        "w_bias_start": draw_w_bias_start(jax.random.fold_in(arg_keys[8], 71), 0),
        "w_out_start": bell_draw(arg_keys[4], (HEADS * HEAD_DIM, C), (HEADS * HEAD_DIM) ** -0.5, 0.5),
        "w_proj_end": bell_draw(arg_keys[5], (C, HEADS * 4 * HEAD_DIM), C ** -0.5, 0.5),
        "w_bias_end": draw_w_bias_end(jax.random.fold_in(arg_keys[8], 71), 0),
        "w_out_end": bell_draw(arg_keys[7], (HEADS * HEAD_DIM, C), (HEADS * HEAD_DIM) ** -0.5, 0.5),
    }


norm_eps = 1e-05
masked_score = -1000000000.0

def layer_norm(features):
    average = lax.optimization_barrier(jnp.mean(features, axis=-1, keepdims=True))
    centred = features - average
    spread = lax.optimization_barrier(jnp.mean(centred * centred, axis=-1, keepdims=True))
    return (centred * lax.rsqrt(spread + norm_eps)).astype(jnp.bfloat16)

def attend(projected, pair_bias, row_ok, key_ok):
    inv_root = HEAD_DIM ** (-0.5)

    def one_row(item_pair):
        packed, valid_row = item_pair
        packed = packed.reshape(N, HEADS, 4, HEAD_DIM).astype(jnp.float32)
        queries = packed[:, :, 0]
        keyset = packed[:, :, 1]
        values = packed[:, :, 2]
        gating = packed[:, :, 3]
        scores = jnp.einsum('bhd,khd->hbk', queries, keyset) * inv_root + pair_bias
        allowed = jnp.logical_and(valid_row, key_ok)
        scores = jnp.where(allowed[None, None, :], scores, masked_score)
        weights = jax.nn.softmax(scores, axis=-1).astype(jnp.bfloat16).astype(jnp.float32)
        summed = jnp.einsum('hbk,khd->bhd', weights, values)
        gated = (jax.nn.sigmoid(gating) * summed).astype(jnp.bfloat16)
        return gated.reshape(N, HEADS * HEAD_DIM)
    return lax.map(one_row, (projected, row_ok))

def start_node(features, residue_ok, w_proj, w_bias, w_out):
    normed = layer_norm(features)
    projected = jnp.dot(normed.reshape(N * N, C), w_proj, preferred_element_type=jnp.float32)
    projected = projected.astype(jnp.bfloat16).reshape(N, N, HEADS * 4 * HEAD_DIM)
    pair_bias = jnp.einsum('abc,ch->hab', normed.astype(jnp.float32), w_bias.astype(jnp.float32))
    gated = attend(projected, pair_bias, residue_ok, residue_ok)
    result = jnp.dot(gated.reshape(N * N, HEADS * HEAD_DIM), w_out, preferred_element_type=jnp.float32)
    return result.astype(jnp.bfloat16).reshape(N, N, C)

def reference(pair_act, residue_mask, w_proj_start, w_bias_start, w_out_start, w_proj_end, w_bias_end, w_out_end):
    residue_ok = residue_mask > 0
    update_start = start_node(pair_act.astype(jnp.float32), residue_ok, w_proj_start, w_bias_start, w_out_start)
    updated = pair_act.astype(jnp.float32) + update_start.astype(jnp.float32)
    flipped = jnp.transpose(updated, (1, 0, 2))
    update_end = start_node(flipped, residue_ok, w_proj_end, w_bias_end, w_out_end)
    update_end = jnp.transpose(update_end, (1, 0, 2))
    return (update_start, update_end)
```

```python
import functools

import jax
import jax.numpy as jnp
from jax import lax
from jax.experimental import pallas as pl
from jax.experimental.pallas import tpu as pltpu
from jax.sharding import PartitionSpec as P

norm_eps = 1e-05
log2e = 1.4426950408889634
far_below = -1e30
lanes = 128


def layer_norm(features):
    average = jnp.mean(features, axis=-1, keepdims=True)
    centred = features - average
    spread = jnp.mean(centred * centred, axis=-1, keepdims=True)
    return (centred * lax.rsqrt(spread + norm_eps)).astype(jnp.bfloat16)


def pack_projection(w_proj, head_count, head_dim):
    split = w_proj.reshape(w_proj.shape[0], head_count, 4, head_dim)
    twice = jnp.concatenate([split, split], axis=-1)
    parts = [twice[:, :, 0], twice[:, :, 1], split[:, :, 2], split[:, :, 3]]
    return jnp.concatenate([part.reshape(w_proj.shape[0], -1) for part in parts], axis=1)


def attend_kernel(
    row_ok_ref,
    key_ok_ref,
    x_ref,
    bias_ref,
    w_proj_ref,
    w_out_ref,
    *rest,
    head_count,
    head_dim,
    query_block,
    bias_swapped,
    emit_next,
):
    if emit_next:
        upd_ref, next_ref, bias_scr = rest
    else:
        upd_ref, bias_scr = rest
    length, channels = x_ref.shape[1], x_ref.shape[2]
    width = head_count * head_dim
    pair = 2 * width
    step = pl.program_id(0)

    @pl.when(step == 0)
    def _():
        allowed = key_ok_ref[...] > 0
        for h in range(head_count):
            plane = bias_ref[h]
            if bias_swapped:
                plane = plane.T
            bias_scr[h] = jnp.where(allowed, plane * log2e, far_below)

    if emit_next:
        features = x_ref[0].astype(jnp.float32)
        normed = layer_norm(features)
    else:
        normed = x_ref[0]
    projected = jnp.dot(normed, w_proj_ref[...], preferred_element_type=jnp.float32).astype(
        jnp.bfloat16
    )
    queries = projected[:, :pair].astype(jnp.float32) * (head_dim ** (-0.5) * log2e)
    keyset = projected[:, pair : 2 * pair]
    values = projected[:, 2 * pair : 2 * pair + width]
    gating = jax.nn.sigmoid(projected[:, 2 * pair + width :].astype(jnp.float32))

    def finish(summed):
        gated = (gating * summed).astype(jnp.bfloat16)
        update = jnp.dot(gated, w_out_ref[...], preferred_element_type=jnp.float32).astype(
            jnp.bfloat16
        )
        upd_ref[0] = update
        if emit_next:
            next_ref[0] = layer_norm(features + update.astype(jnp.float32))

    row_ok = row_ok_ref[step] > 0

    @pl.when(row_ok)
    def _():
        upper = queries.astype(jnp.bfloat16)
        lower = (queries - upper.astype(jnp.float32)).astype(jnp.bfloat16)
        spot = lax.broadcasted_iota(jnp.int32, (1, pair), 1)
        both = jnp.where(spot % (2 * head_dim) < head_dim, upper, lower)
        values_ones = jnp.concatenate([values, jnp.ones_like(values)], axis=1)
        owner = lax.broadcasted_iota(jnp.int32, (1, width), 1) // head_dim
        block_heads = lanes // (2 * head_dim)
        pieces = []
        for start in range(0, length, query_block):
            summed = jnp.zeros((query_block, width), jnp.float32)
            for h in range(head_count):
                base = h // block_heads * lanes
                local = lax.broadcasted_iota(jnp.int32, (1, lanes), 1) // (2 * head_dim)
                lhs = jnp.where(
                    local == h % block_heads,
                    both[start : start + query_block, base : base + lanes],
                    jnp.zeros((), jnp.bfloat16),
                )
                scores = lax.dot_general(
                    lhs,
                    keyset[:, base : base + lanes],
                    (((1,), (1,)), ((), ())),
                    preferred_element_type=jnp.float32,
                )
                scores = scores + bias_scr[h, start : start + query_block]
                top = jnp.max(scores, axis=-1, keepdims=True)
                weights = jnp.exp2(scores - top).astype(jnp.bfloat16)
                both_sums = jnp.dot(weights, values_ones, preferred_element_type=jnp.float32)
                ratio = both_sums[:, :width] / both_sums[:, width:]
                summed = jnp.where(owner == h, ratio, summed)
            pieces.append(summed)
        finish(jnp.concatenate(pieces, axis=0))

    @pl.when(jnp.logical_not(row_ok))
    def _():
        even = jnp.full((), 1.0 / length, jnp.float32).astype(jnp.bfloat16).astype(jnp.float32)
        total = jnp.sum(values.astype(jnp.float32), axis=0, keepdims=True)
        finish(jnp.broadcast_to(total * even, (length, width)))


def attend(row_ok, key_ok, lines, pair_bias, w_proj, w_out, bias_swapped, emit_next):
    count, length, channels = lines.shape
    head_count = pair_bias.shape[0]
    width = w_out.shape[0]
    head_dim = width // head_count
    query_block = min(length, 256)
    packed = pack_projection(w_proj, head_count, head_dim)
    line_spec = pl.BlockSpec((1, length, channels), lambda i, ok: (i, 0, 0))

    def whole(shape):
        return pl.BlockSpec(shape, lambda i, ok: (0,) * len(shape), pipeline_mode=pl.Buffered(1))

    out_count = 2 if emit_next else 1
    line_shape = jax.ShapeDtypeStruct((count, length, channels), jnp.bfloat16)
    scores = count * head_count * length * length
    return pl.pallas_call(
        functools.partial(
            attend_kernel,
            head_count=head_count,
            head_dim=head_dim,
            query_block=query_block,
            bias_swapped=bias_swapped,
            emit_next=emit_next,
        ),
        out_shape=[line_shape] * out_count,
        grid_spec=pltpu.PrefetchScalarGridSpec(
            num_scalar_prefetch=1,
            grid=(count,),
            in_specs=[
                whole((1, length)),
                line_spec,
                whole((head_count, length, length)),
                whole(packed.shape),
                whole(w_out.shape),
            ],
            out_specs=[line_spec] * out_count,
            scratch_shapes=[pltpu.VMEM((head_count, length, length), jnp.float32)],
        ),
        compiler_params=pltpu.CompilerParams(
            dimension_semantics=("arbitrary",), vmem_limit_bytes=56 * 1024 * 1024
        ),
        cost_estimate=pl.CostEstimate(
            flops=4 * scores * 128, bytes_accessed=8 * lines.size, transcendentals=scores
        ),
        name="attend_next" if emit_next else "attend_last",
    )(row_ok, key_ok[None, :], lines, pair_bias, packed, w_out)


def on_device(
    pair_act,
    residue_mask,
    w_proj_start,
    w_bias_start,
    w_out_start,
    w_proj_end,
    w_bias_end,
    w_out_end,
):
    wide_count = lax.axis_size("wide")
    narrow_count = lax.axis_size("narrow")
    wide_at = lax.axis_index("wide")
    narrow_at = lax.axis_index("narrow")
    tile_rows, tile_cols, channels = pair_act.shape
    row_count = tile_rows // narrow_count
    col_count = tile_cols // wide_count
    mask = (residue_mask > 0).astype(jnp.int32)

    rows = lax.all_to_all(pair_act, "narrow", split_axis=0, concat_axis=1, tiled=True)
    normed = layer_norm(rows.astype(jnp.float32))
    bias_part = jnp.einsum("abc,ch->hab", normed, w_bias_start, preferred_element_type=jnp.float32)
    pair_bias = lax.all_gather(bias_part, ("wide", "narrow"), axis=1, tiled=True)
    row_ok = lax.dynamic_slice_in_dim(mask, wide_at * tile_rows + narrow_at * row_count, row_count)
    upd_rows, next_rows = attend(
        row_ok, mask, rows, pair_bias, w_proj_start, w_out_start, False, True
    )
    update_start = lax.all_to_all(upd_rows, "narrow", split_axis=1, concat_axis=0, tiled=True)

    bias_part_end = jnp.einsum(
        "abc,ch->hab", next_rows, w_bias_end, preferred_element_type=jnp.float32
    )
    pair_bias_end = lax.all_gather(bias_part_end, ("wide", "narrow"), axis=1, tiled=True)
    next_tile = lax.all_to_all(next_rows, "narrow", split_axis=1, concat_axis=0, tiled=True)
    columns = lax.all_to_all(
        next_tile.transpose(1, 0, 2), "wide", split_axis=0, concat_axis=1, tiled=True
    )
    col_ok = lax.dynamic_slice_in_dim(mask, narrow_at * tile_cols + wide_at * col_count, col_count)
    (upd_cols,) = attend(
        col_ok, mask, columns, pair_bias_end, w_proj_end, w_out_end, True, False
    )
    upd_tile = lax.all_to_all(upd_cols, "wide", split_axis=1, concat_axis=0, tiled=True)
    return (update_start, upd_tile.transpose(1, 0, 2))


def solution(mesh):
    in_specs = (P("wide", "narrow", None), P(), P(), P(), P(), P(), P(), P())
    out_specs = (P("wide", "narrow", None), P("wide", "narrow", None))
    return jax.shard_map(
        on_device, mesh=mesh, in_specs=in_specs, out_specs=out_specs, check_vma=False
    )
```

```python
import functools

import jax
import jax.numpy as jnp
from jax import lax
from jax.experimental import pallas as pl
from jax.experimental.pallas import tpu as pltpu
from jax.sharding import PartitionSpec as P


norm_eps = 1e-05
log2e = 1.4426950408889634
far_below = -1e30
lanes = 128
both_axes = ("wide", "narrow")


def params(megabytes=60):
    return pltpu.CompilerParams(
        dimension_semantics=("arbitrary",), vmem_limit_bytes=megabytes * 1024 * 1024
    )


def once(shape):
    return pl.BlockSpec(
        shape, lambda *_: (0,) * len(shape), pipeline_mode=pl.Buffered(1)
    )


def layer_norm(features):
    average = jnp.mean(features, axis=-1, keepdims=True)
    centred = features - average
    spread = jnp.mean(centred * centred, axis=-1, keepdims=True)
    return (centred * lax.rsqrt(spread + norm_eps)).astype(jnp.bfloat16)


def pack_projection(w_proj, head_count, head_dim):
    split = w_proj.reshape(w_proj.shape[0], head_count, 4, head_dim)
    twice = jnp.concatenate([split, split], axis=-1)
    parts = [twice[:, :, 1], split[:, :, 2], twice[:, :, 0], split[:, :, 3]]
    return jnp.concatenate([part.reshape(w_proj.shape[0], -1) for part in parts], axis=1)


def tile_bias_kernel(x_ref, w_ref, out_ref, *, head_count):
    for i in range(x_ref.shape[0]):
        normed = layer_norm(x_ref[i].astype(jnp.float32))
        got = lax.dot_general(
            w_ref[...], normed, (((1,), (1,)), ((), ())), preferred_element_type=jnp.float32
        )
        for h in range(head_count):
            out_ref[h, i : i + 1, :] = got[h : h + 1]


def tile_bias(tile, w_bias_rows, head_count):
    rows, cols, channels = tile.shape
    block = 8 if rows % 8 == 0 else rows
    return pl.pallas_call(
        functools.partial(tile_bias_kernel, head_count=head_count),
        out_shape=jax.ShapeDtypeStruct((head_count, rows, cols), jnp.float32),
        grid=(rows // block,),
        in_specs=[
            pl.BlockSpec((block, cols, channels), lambda i: (i, 0, 0)),
            once(w_bias_rows.shape),
        ],
        out_specs=pl.BlockSpec((head_count, block, cols), lambda i: (0, i, 0)),
        compiler_params=params(16),
        cost_estimate=pl.CostEstimate(
            flops=32 * tile.size, bytes_accessed=2 * tile.size, transcendentals=0
        ),
        name="tile_bias",
    )(tile, w_bias_rows)


def pack_tile_bias(part):
    rows, cols = part.shape[1:]
    main = cols // lanes * lanes
    left, right = part[:, :, :main], part[:, :, main:]
    half = rows // 2
    tail = jnp.concatenate([right[:, :half], right[:, half:]], axis=2)
    split = [left[:, :, at : at + lanes] for at in range(0, main, lanes)]
    return jnp.concatenate(split + [tail], axis=1)


def place_bias_kernel(key_ok_ref, got_ref, out_ref, *, rows, cols):
    main = cols // lanes
    half_lanes = lanes // 2
    low = lax.broadcasted_iota(jnp.int32, (1, lanes), 1) < half_lanes
    for n in range(0, got_ref.shape[0], 2):
        for h in range(got_ref.shape[1]):
            blocks = []
            even = [got_ref[n, h, b * rows : (b + 1) * rows] for b in range(main)]
            odd = [got_ref[n + 1, h, b * rows : (b + 1) * rows] for b in range(main)]
            even_tail = got_ref[n, h, main * rows :]
            odd_tail = got_ref[n + 1, h, main * rows :]
            even_last = jnp.concatenate(
                [even_tail, pltpu.roll(even_tail, half_lanes, 1)], axis=0
            )
            odd_last = jnp.concatenate([pltpu.roll(odd_tail, half_lanes, 1), odd_tail], axis=0)
            turned = [pltpu.roll(piece, half_lanes, 1) for piece in odd]
            blocks = list(even)
            before = even_last
            for piece in turned:
                blocks.append(jnp.where(low, before, piece))
                before = piece
            blocks.append(jnp.where(low, before, odd_last))
            for at, block in enumerate(blocks):
                lane = n * cols + at * lanes
                allowed = key_ok_ref[:, lane : lane + lanes] > 0
                out_ref[h, :, lane : lane + lanes] = jnp.where(allowed, block * log2e, far_below)


def place_bias(key_ok, gathered, wide_count, rows, cols):
    narrow_count = gathered.shape[0] // wide_count
    head_count = gathered.shape[1]
    length = wide_count * rows
    return pl.pallas_call(
        functools.partial(place_bias_kernel, rows=rows, cols=cols),
        out_shape=jax.ShapeDtypeStruct((head_count, length, length), jnp.float32),
        grid=(wide_count,),
        in_specs=[
            once((1, length)),
            pl.BlockSpec((narrow_count,) + gathered.shape[1:], lambda i: (i, 0, 0, 0)),
        ],
        out_specs=pl.BlockSpec((head_count, rows, length), lambda i: (0, i, 0)),
        compiler_params=params(16),
        cost_estimate=pl.CostEstimate(
            flops=gathered.size, bytes_accessed=8 * gathered.size, transcendentals=0
        ),
        name="place_bias",
    )(key_ok[None, :], gathered)


def turn_bias_kernel(key_ok_ref, got_ref, out_ref):
    queries = got_ref.shape[-1]
    plane = got_ref[:, 0, 0].reshape(-1, queries)
    allowed = key_ok_ref[...] > 0
    out_ref[0] = jnp.where(allowed, plane.T * log2e, far_below)


def turn_bias(key_ok, gathered, part):
    devices, _, head_count, rows, queries = gathered.shape
    length = devices * rows
    return pl.pallas_call(
        turn_bias_kernel,
        out_shape=jax.ShapeDtypeStruct((head_count, queries, length), jnp.float32),
        grid=(head_count,),
        in_specs=[
            once((1, length)),
            pl.BlockSpec((devices, 1, 1, rows, queries), lambda h: (0, part, h, 0, 0)),
        ],
        out_specs=pl.BlockSpec((1, queries, length), lambda h: (h, 0, 0)),
        compiler_params=params(),
        cost_estimate=pl.CostEstimate(
            flops=gathered.size, bytes_accessed=8 * gathered.size, transcendentals=0
        ),
        name="turn_bias",
    )(key_ok[None, :], gathered)


def lines_per_step(count, most):
    return max(per for per in range(1, most + 1) if count % per == 0)


def project_kernel(x_ref, w_ref, *rest, head_count, head_dim, normalise, strided):
    out_ref, scratch = (rest[-2], rest[-1]) if strided else (rest[-1], None)
    width = head_count * head_dim
    pair = 2 * width
    channels = x_ref.shape[-1]
    per = out_ref.shape[0]
    if strided:
        stride = x_ref.shape[1]

        @pl.when(pl.program_id(0) == 0)
        def _():
            scratch[...] = x_ref[...].astype(jnp.float32).reshape(scratch.shape)

    for i in range(per):
        if strided:
            at = pl.program_id(0) * per + i
            normed = scratch[pl.ds(at, x_ref.shape[0], stride=stride), :].astype(jnp.bfloat16)
        elif normalise:
            normed = layer_norm(x_ref[:, i].reshape(-1, channels).astype(jnp.float32))
        else:
            normed = x_ref[i]
        projected = jnp.dot(normed, w_ref[...], preferred_element_type=jnp.float32).astype(
            jnp.bfloat16
        )
        first = pair + width
        queries = projected[:, first : first + pair].astype(jnp.float32)
        queries = queries * (head_dim ** (-0.5) * log2e)
        upper = queries.astype(jnp.bfloat16)
        lower = (queries - upper.astype(jnp.float32)).astype(jnp.bfloat16)
        spot = lax.broadcasted_iota(jnp.int32, (1, pair), 1)
        queries = jnp.where(spot % (2 * head_dim) < head_dim, upper, lower)
        for block in range(projected.shape[1] // lanes):
            at = block * lanes
            if first <= at < first + pair:
                out_ref[i, block] = queries[:, at - first : at - first + lanes]
            else:
                out_ref[i, block] = projected[:, at : at + lanes]


def project(lines, packed, head_count, head_dim, kind, before=None, first=0, total=None):
    channels = lines.shape[-1]
    scratch = []
    if kind == "rows":
        pieces, count, cols = lines.shape[:3]
        length = pieces * cols
        per = lines_per_step(count, 2)
        spec = pl.BlockSpec((pieces, per, cols, channels), lambda i: (0, i, 0, 0))
    elif kind == "columns":
        length, count = lines.shape[:2]
        per = lines_per_step(count, 2)
        spec = once(lines.shape)
        scratch = [pltpu.VMEM((length * count, channels), jnp.float32)]
    else:
        count, length = lines.shape[:2]
        per = 1
        spec = pl.BlockSpec((1, length, channels), lambda i: (i, 0, 0))
    outs = packed.shape[1]
    total = count if total is None else total
    in_specs, operands, aliases = [spec, once(packed.shape)], [lines, packed], {}
    if before is not None:
        in_specs.append(pl.BlockSpec(memory_space=pl.ANY))
        operands.append(before)
        aliases = {2: 0}
    skip = first // per
    return pl.pallas_call(
        functools.partial(
            project_kernel,
            head_count=head_count,
            head_dim=head_dim,
            normalise=kind == "rows",
            strided=kind == "columns",
        ),
        out_shape=jax.ShapeDtypeStruct((total, outs // lanes, length, lanes), jnp.bfloat16),
        grid=(count // per,),
        in_specs=in_specs,
        out_specs=pl.BlockSpec((per, outs // lanes, length, lanes), lambda i: (i + skip, 0, 0, 0)),
        scratch_shapes=scratch,
        input_output_aliases=aliases,
        compiler_params=params(),
        cost_estimate=pl.CostEstimate(
            flops=2 * lines.size * outs,
            bytes_accessed=2 * lines.size * (1 + outs // channels),
            transcendentals=0,
        ),
    )(*operands)


def attend_lines(query_ref, key_ref, bias_refs, oks, head_count, head_dim):
    width = head_count * head_dim
    pair_blocks = 2 * width // lanes
    length = key_ref.shape[2]
    local = lax.broadcasted_iota(jnp.int32, (1, lanes), 1) // (2 * head_dim)
    owner = lax.broadcasted_iota(jnp.int32, (1, width), 1) // head_dim
    block_heads = lanes // (2 * head_dim)
    nothing = jnp.zeros((), jnp.bfloat16)
    jobs = [
        (i, at, h)
        for i in range(key_ref.shape[0])
        for at in range(len(bias_refs))
        for h in range(head_count)
    ]

    def score(job):
        i, at, h = job
        block = h // block_heads
        queries = query_ref[i, block, :, at].reshape(-1, lanes)
        return lax.dot_general(
            jnp.where(local == h % block_heads, queries, nothing),
            key_ref[i, block],
            (((1,), (1,)), ((), ())),
            preferred_element_type=jnp.float32,
        )

    def together(ref, i, first, *rest):
        parts = [ref[(i, first + n) + rest] for n in range(width // lanes)]
        parts = [part.reshape(-1, lanes) for part in parts]
        return parts[0] if len(parts) == 1 else jnp.concatenate(parts, axis=1)

    gated = {}
    summed = None
    coming = score(jobs[0])
    for n, (i, at, h) in enumerate(jobs):
        scores = coming
        if n + 1 < len(jobs):
            coming = score(jobs[n + 1])
        scores = scores + bias_refs[at][h].reshape(-1, length)
        top = jnp.max(scores, axis=-1, keepdims=True)
        weights = jnp.exp2(scores - top).astype(jnp.bfloat16)
        values = together(key_ref, i, pair_blocks)
        values_ones = jnp.concatenate([values, jnp.ones_like(values)], axis=1)
        both_sums = jnp.dot(weights, values_ones, preferred_element_type=jnp.float32)
        ratio = both_sums[:, :width] / both_sums[:, width:]
        summed = ratio if h == 0 else jnp.where(owner == h, ratio, summed)
        if h == head_count - 1:
            even = jnp.full((), 1.0 / length, jnp.float32).astype(jnp.bfloat16)
            total = jnp.sum(values.astype(jnp.float32), axis=0, keepdims=True)
            final = jnp.where(oks[i], summed, total * even.astype(jnp.float32))
            gates = together(query_ref, i, pair_blocks, slice(None), at).astype(jnp.float32)
            gated[i, at] = (jax.nn.sigmoid(gates) * final).astype(jnp.bfloat16)
    return gated


def out_of(gated, w_out_ref):
    return jnp.dot(gated, w_out_ref[...], preferred_element_type=jnp.float32).astype(jnp.bfloat16)


def attend_rows_kernel(
    row_ok_ref, query_ref, key_ref, bias_ref, w_out_ref, x_ref, w_bias_ref, *rest, **sizes
):
    upd_ref, next_ref, nbias_ref = rest[-3:]
    per = key_ref.shape[0]
    lines = [pl.program_id(0) * per + i for i in range(per)]
    oks = [row_ok_ref[line] > 0 for line in lines]
    gated = attend_lines(query_ref, key_ref, [bias_ref], oks, **sizes)
    for i in range(per):
        update = out_of(gated[i, 0], w_out_ref)
        upd_ref[:, i] = update.reshape(upd_ref.shape[0], *upd_ref.shape[2:])
        features = x_ref[:, i].reshape(-1, x_ref.shape[-1]).astype(jnp.float32)
        normed = layer_norm(features + update.astype(jnp.float32))
        got = lax.dot_general(
            w_bias_ref[...], normed, (((1,), (1,)), ((), ())), preferred_element_type=jnp.float32
        )
        for h in range(nbias_ref.shape[0]):
            nbias_ref[h, pl.ds(lines[i], 1), :] = got[h : h + 1]
        if len(next_ref.shape) == 4:
            devices, _, cols, channels = next_ref.shape
            narrow_count = upd_ref.shape[0]
            spread = normed.astype(jnp.float32).reshape(
                narrow_count, devices // narrow_count, cols, channels
            )
            spread = spread.transpose(1, 0, 2, 3).reshape(devices, cols, channels)
            next_ref[:, i] = spread.astype(jnp.bfloat16)
        else:
            next_ref[i] = normed


def line_specs(projected, plan, per, first, parts, skip):
    blocks, chunks, piece = plan[:3]
    total, lane_blocks, length, _ = projected.shape
    half = lane_blocks // 2
    cut = projected.reshape(total, lane_blocks, blocks, chunks, piece, lanes)
    at = first // parts
    specs = [
        pl.BlockSpec(
            (per, half, blocks, parts, piece, lanes), lambda i, ok: (i + skip, 1, 0, at, 0, 0)
        ),
        pl.BlockSpec((per, half, length, lanes), lambda i, ok: (i + skip, 0, 0, 0)),
    ]
    return specs, [cut, projected]


def attend_rows(row_ok, projected, lines, bias, w_out, w_bias_rows, chunk, before, plan):
    blocks, chunks, piece, own, wide_count = plan
    pieces, count, cols, channels = lines.shape
    length = pieces * cols
    head_count = bias.shape[0]
    width = w_out.shape[0]
    head_dim = width // head_count
    direct = own % 8 == 0
    inner = blocks // pieces
    x_cut = lines.reshape(pieces, count, inner, chunks, piece, channels)
    bias_cut = bias.reshape(head_count, blocks, chunks, piece, length)
    per = lines_per_step(count, 2)
    queries = blocks * piece
    line_block = pl.BlockSpec(
        (pieces, per, inner, None, piece, channels), lambda i, ok: (0, i, 0, chunk, 0, 0)
    )
    if direct:
        next_shape = (wide_count * pieces, count, own, channels)
        next_spec = pl.BlockSpec(
            (wide_count * pieces, per, own, channels), lambda i, ok: (0, i, 0, 0)
        )
    else:
        next_shape = (count, queries, channels)
        next_spec = pl.BlockSpec((per, queries, channels), lambda i, ok: (i, 0, 0))
    nbias_shape = (head_count, count, queries)
    scores = count * head_count * length * queries
    in_specs, operands = line_specs(projected, plan, per, chunk, 1, 0)
    in_specs += [
        pl.BlockSpec(
            (head_count, blocks, None, piece, length),
            lambda i, ok: (0, 0, chunk, 0, 0),
            pipeline_mode=pl.Buffered(1),
        ),
        once(w_out.shape),
        line_block,
        once(w_bias_rows.shape),
    ]
    operands += [bias_cut, w_out, x_cut, w_bias_rows]
    aliases = {}
    if before is not None:
        in_specs.append(pl.BlockSpec(memory_space=pl.ANY))
        operands.append(before)
        aliases = {len(operands): 0}
    upd, nxt, nbias = pl.pallas_call(
        functools.partial(attend_rows_kernel, head_count=head_count, head_dim=head_dim),
        out_shape=[
            jax.ShapeDtypeStruct(x_cut.shape, jnp.bfloat16),
            jax.ShapeDtypeStruct(next_shape, jnp.bfloat16),
            jax.ShapeDtypeStruct(nbias_shape, jnp.float32),
        ],
        grid_spec=pltpu.PrefetchScalarGridSpec(
            num_scalar_prefetch=1,
            grid=(count // per,),
            in_specs=in_specs,
            out_specs=[line_block, next_spec, pl.BlockSpec(nbias_shape, lambda i, ok: (0, 0, 0))],
        ),
        input_output_aliases=aliases,
        compiler_params=params(),
        cost_estimate=pl.CostEstimate(
            flops=4 * scores * 128, bytes_accessed=8 * lines.size, transcendentals=scores
        ),
        name="attend_rows",
    )(row_ok, *operands)
    if not direct:
        nxt = nxt.reshape(count, pieces, wide_count, own, channels).transpose(2, 1, 0, 3, 4)
        nxt = nxt.reshape(wide_count * pieces, count, own, channels)
    return upd, nxt, nbias


def attend_columns_kernel(col_ok_ref, query_ref, key_ref, *rest, parts, **sizes):
    bias_refs, w_out_ref, out_ref = rest[:parts], rest[parts], rest[parts + 1]
    scratch = rest[parts + 2 :]
    per = key_ref.shape[0]
    blocks, piece = query_ref.shape[2], query_ref.shape[4]
    lines = [pl.program_id(0) * per + i for i in range(per)]
    oks = [col_ok_ref[line] > 0 for line in lines]
    gated = attend_lines(query_ref, key_ref, bias_refs, oks, **sizes)
    for i in range(per):
        for at in range(parts):
            update = out_of(gated[i, at], w_out_ref)
            if not scratch:
                out_ref[:, i] = update.reshape(blocks, piece, update.shape[1])
                continue
            stride = out_ref.shape[2]
            for m in range(blocks):
                first = (m * parts + at) * piece * stride + lines[i]
                scratch[0][pl.ds(first, piece, stride=stride), :] = update[
                    m * piece : (m + 1) * piece
                ].astype(jnp.float32)
    if scratch:

        @pl.when(pl.program_id(0) == pl.num_programs(0) - 1)
        def _():
            out_ref[...] = scratch[0][...].reshape(out_ref.shape).astype(jnp.bfloat16)


def attend_columns(col_ok, projected, biases, w_out, first, skip, plan):
    blocks, _, piece, own, _ = plan
    length = projected.shape[2]
    count = col_ok.shape[0]
    parts = len(biases)
    head_count = biases[0].shape[0]
    width = w_out.shape[0]
    head_dim = width // head_count
    scores = count * head_count * length * blocks * parts * piece
    per = lines_per_step(count, 2) if parts == 1 else 1
    if own % 8 == 0:
        out_shape = (blocks, parts * piece, count, width)
        out_spec = pl.BlockSpec(out_shape, lambda i, ok: (0, 0, 0, 0))
        scratch = [pltpu.VMEM((blocks * parts * piece * count, width), jnp.float32)]
    else:
        out_shape = (blocks, count, parts * piece, width)
        out_spec = pl.BlockSpec((blocks, per, parts * piece, width), lambda i, ok: (0, i, 0, 0))
        scratch = []
    in_specs, operands = line_specs(projected, plan, per, first, parts, skip // per)
    return pl.pallas_call(
        functools.partial(
            attend_columns_kernel, parts=parts, head_count=head_count, head_dim=head_dim
        ),
        out_shape=jax.ShapeDtypeStruct(out_shape, jnp.bfloat16),
        grid_spec=pltpu.PrefetchScalarGridSpec(
            num_scalar_prefetch=1,
            grid=(count // per,),
            in_specs=in_specs + [once(biases[0].shape)] * parts + [once(w_out.shape)],
            out_specs=out_spec,
            scratch_shapes=scratch,
        ),
        compiler_params=params(),
        cost_estimate=pl.CostEstimate(
            flops=4 * scores * 128, bytes_accessed=8 * count * length * width, transcendentals=scores
        ),
        name="attend_columns",
    )(col_ok, *operands, *biases, w_out)


def settle_kernel(*refs, order, plan):
    _, chunks, piece, own, wide_count = plan
    tile_rows = chunks * piece
    out_ref = refs[-1]
    for step, j in enumerate(order):
        ref, first = (refs[0], step * own) if len(refs) < chunks else (refs[step], 0)
        for w in range(wide_count):
            inner, within = divmod(w * own, piece)
            col = inner * tile_rows + j * piece + within
            out_ref[:, col : col + own, :] = ref[w, :, first : first + own, :]


def settle(parts, first_row, before, order, plan, shape):
    wide_count, rows, _, _ = parts[0].shape
    block = 16
    skip = first_row // block
    in_specs = [
        pl.BlockSpec((wide_count, block) + part.shape[2:], lambda i: (0, i, 0, 0))
        for part in parts
    ]
    operands, aliases = list(parts), {}
    if before is not None:
        in_specs.append(pl.BlockSpec(memory_space=pl.ANY))
        operands.append(before)
        aliases = {len(parts): 0}
    return pl.pallas_call(
        functools.partial(settle_kernel, order=order, plan=plan),
        out_shape=jax.ShapeDtypeStruct(shape, jnp.bfloat16),
        grid=(rows // block,),
        in_specs=in_specs,
        out_specs=pl.BlockSpec((block,) + shape[1:], lambda i: (i + skip, 0, 0)),
        input_output_aliases=aliases,
        compiler_params=params(),
        cost_estimate=pl.CostEstimate(
            flops=0, bytes_accessed=4 * parts[0].size * len(parts), transcendentals=0
        ),
        name="settle",
    )(*operands)


def bias_rows_of(w_bias):
    turned = w_bias.T
    return jnp.pad(turned, ((0, 16 - turned.shape[0]), (0, 0)))


def on_device(
    pair_act,
    residue_mask,
    w_proj_start,
    w_bias_start,
    w_out_start,
    w_proj_end,
    w_bias_end,
    w_out_end,
):
    wide_count = lax.axis_size("wide")
    narrow_count = lax.axis_size("narrow")
    wide_at = lax.axis_index("wide")
    narrow_at = lax.axis_index("narrow")
    tile_rows, tile_cols, channels = pair_act.shape
    head_count = w_bias_start.shape[1]
    head_dim = w_out_start.shape[0] // head_count
    length = wide_count * tile_rows
    row_count = tile_rows // narrow_count
    chunks = 1
    if tile_cols % tile_rows == 0:
        for tried in (3, 2):
            if tile_rows % (16 * tried) == 0 and tile_cols % (8 * tried * wide_count) == 0:
                chunks = tried
                break
    piece = tile_rows // chunks
    own = tile_cols // chunks // wide_count
    plan = (wide_count, chunks, piece, own, wide_count)
    key_ok = (residue_mask > 0).astype(jnp.int32)

    part = tile_bias(pair_act, bias_rows_of(w_bias_start), head_count)
    dense = tile_cols % lanes == lanes // 2 and tile_rows % 16 == 0 and narrow_count % 2 == 0
    if dense:
        part = pack_tile_bias(part)
    gathered = lax.all_gather(part, both_axes, axis=0, tiled=False)
    tile_in, part = lax.optimization_barrier((pair_act, part))
    lines = lax.all_to_all(
        tile_in.reshape(narrow_count, row_count, tile_cols, channels),
        "narrow",
        split_axis=0,
        concat_axis=0,
        tiled=True,
    )
    packed_start = pack_projection(w_proj_start, head_count, head_dim)
    projected = project(lines, packed_start, head_count, head_dim, "rows")
    if dense:
        bias = place_bias(key_ok, gathered, wide_count, tile_rows, tile_cols)
    else:
        bias = gathered.reshape(wide_count, narrow_count, head_count, tile_rows, tile_cols)
        bias = bias.transpose(2, 0, 3, 1, 4).reshape(head_count, length, length)
        bias = jnp.where(key_ok > 0, bias * log2e, far_below)

    row_ok = lax.dynamic_slice_in_dim(
        key_ok, wide_at * tile_rows + narrow_at * row_count, row_count
    )
    w_bias_rows = bias_rows_of(w_bias_end)
    order = [chunks - 1] + list(range(chunks - 1))
    columns, waiting, next_biases = {}, [], {}
    upd = None
    for step, j in enumerate(order):
        upd, nxt, nbias = attend_rows(
            row_ok, projected, lines, bias, w_out_start, w_bias_rows, j, upd, plan
        )
        waiting.append((j, nbias))
        if step in (0, chunks - 1):
            got = lax.all_gather(
                jnp.stack([nbias for _, nbias in waiting]), both_axes, axis=0, tiled=False
            )
            for n, (k, _) in enumerate(waiting):
                if row_count % 8 == 0:
                    turned = turn_bias(key_ok, got, n)
                else:
                    turned = got[:, n].transpose(1, 3, 0, 2).reshape(head_count, -1, length)
                    turned = jnp.where(key_ok > 0, turned * log2e, far_below)
                next_biases[k] = turned
            waiting = []
        got = lax.all_to_all(nxt, both_axes, split_axis=0, concat_axis=0, tiled=True)
        columns[j] = got.reshape(length, own, channels)
    mine = upd.reshape(narrow_count, row_count, tile_cols, channels)
    leaving = [
        lax.dynamic_index_in_dim(mine, (narrow_at + k) % narrow_count, 0)
        for k in range(1, narrow_count)
    ]
    leaving, mine = lax.optimization_barrier((leaving, mine))
    arrived = []
    for k in range(1, narrow_count):
        ring = [(n, (n + k) % narrow_count) for n in range(narrow_count)]
        arrived.append(lax.ppermute(leaving[k - 1], "narrow", ring))
    update_start = mine
    for k, got in enumerate(arrived, 1):
        source = (narrow_at + narrow_count - k) % narrow_count
        update_start = lax.dynamic_update_slice_in_dim(update_start, got, source, 0)
    update_start = update_start.reshape(tile_rows, tile_cols, channels)

    packed_end = pack_projection(w_proj_end, head_count, head_dim)
    projected_end, col_ok = None, []
    for step, j in enumerate(order):
        lines_end = columns[j]
        if own % 8:
            lines_end = lines_end.transpose(1, 0, 2)
        projected_end = project(
            lines_end,
            packed_end,
            head_count,
            head_dim,
            "plain" if own % 8 else "columns",
            projected_end,
            step * own,
            chunks * own,
        )
        at = wide_at * own + jnp.arange(own)
        at = narrow_at * tile_cols + at // piece * tile_rows + j * piece + at % piece
        col_ok.append(key_ok[at])

    got = attend_columns(
        jnp.concatenate(col_ok),
        projected_end,
        [next_biases[order[0]]],
        w_out_end,
        order[0],
        0,
        plan,
    )
    got = lax.all_to_all(got, "wide", split_axis=0, concat_axis=0, tiled=True)
    if chunks == 1:
        return (update_start, got.transpose(2, 0, 1, 3).reshape(pair_act.shape))
    settled = settle([got], (chunks - 1) * piece, None, order, plan, pair_act.shape)
    late = []
    for step, j in enumerate(order):
        got = attend_columns(
            col_ok[step],
            projected_end,
            [next_biases[k] for k in range(chunks - 1)],
            w_out_end,
            0,
            step * own,
            plan,
        )
        late.append(lax.all_to_all(got, "wide", split_axis=0, concat_axis=0, tiled=True))
    return (update_start, settle(late, 0, settled, order, plan, pair_act.shape))


def solution(mesh):
    in_specs = (P("wide", "narrow", None), P(), P(), P(), P(), P(), P(), P())
    out_specs = (P("wide", "narrow", None), P("wide", "narrow", None))
    return jax.shard_map(
        on_device, mesh=mesh, in_specs=in_specs, out_specs=out_specs, check_vma=False
    )
```

```python
import functools

import jax
import jax.numpy as jnp
from jax import lax
from jax.experimental import pallas as pl
from jax.experimental.pallas import tpu as pltpu
from jax.sharding import PartitionSpec as P


norm_eps = 1e-05
log2e = 1.4426950408889634
far_below = -1e30
lanes = 128
both_axes = ("wide", "narrow")


def params(megabytes=60):
    return pltpu.CompilerParams(
        dimension_semantics=("arbitrary",), vmem_limit_bytes=megabytes * 1024 * 1024
    )


def once(shape):
    return pl.BlockSpec(
        shape, lambda *_: (0,) * len(shape), pipeline_mode=pl.Buffered(1)
    )


def layer_norm(features):
    average = jnp.mean(features, axis=-1, keepdims=True)
    centred = features - average
    spread = jnp.mean(centred * centred, axis=-1, keepdims=True)
    return (centred * lax.rsqrt(spread + norm_eps)).astype(jnp.bfloat16)


def pack_projection(w_proj, head_count, head_dim):
    split = w_proj.reshape(w_proj.shape[0], head_count, 4, head_dim)
    twice = jnp.concatenate([split, split], axis=-1)
    parts = [twice[:, :, 1], split[:, :, 2], twice[:, :, 0], split[:, :, 3]]
    return jnp.concatenate([part.reshape(w_proj.shape[0], -1) for part in parts], axis=1)


def tile_bias_kernel(x_ref, w_ref, out_ref, *, head_count):
    for i in range(x_ref.shape[0]):
        normed = layer_norm(x_ref[i].astype(jnp.float32))
        got = lax.dot_general(
            w_ref[...], normed, (((1,), (1,)), ((), ())), preferred_element_type=jnp.float32
        )
        for h in range(head_count):
            out_ref[h, i : i + 1, :] = got[h : h + 1]


def tile_bias(tile, w_bias_rows, head_count):
    rows, cols, channels = tile.shape
    block = 8 if rows % 8 == 0 else rows
    return pl.pallas_call(
        functools.partial(tile_bias_kernel, head_count=head_count),
        out_shape=jax.ShapeDtypeStruct((head_count, rows, cols), jnp.float32),
        grid=(rows // block,),
        in_specs=[
            pl.BlockSpec((block, cols, channels), lambda i: (i, 0, 0)),
            once(w_bias_rows.shape),
        ],
        out_specs=pl.BlockSpec((head_count, block, cols), lambda i: (0, i, 0)),
        compiler_params=params(),
        cost_estimate=pl.CostEstimate(
            flops=32 * tile.size, bytes_accessed=2 * tile.size, transcendentals=0
        ),
        name="tile_bias",
    )(tile, w_bias_rows)


def pack_tile_bias(part):
    rows, cols = part.shape[1:]
    main = cols // lanes * lanes
    left, right = part[:, :, :main], part[:, :, main:]
    half = rows // 2
    tail = jnp.concatenate([right[:, :half], right[:, half:]], axis=2)
    split = [left[:, :, at : at + lanes] for at in range(0, main, lanes)]
    return jnp.concatenate(split + [tail], axis=1)


def place_bias_kernel(key_ok_ref, got_ref, out_ref, *, rows, cols):
    main = cols // lanes
    half_lanes = lanes // 2
    low = lax.broadcasted_iota(jnp.int32, (1, lanes), 1) < half_lanes

    def one_head(h, _):
        for n in range(0, got_ref.shape[0], 2):
            even = [got_ref[n, h, b * rows : (b + 1) * rows] for b in range(main)]
            odd = [got_ref[n + 1, h, b * rows : (b + 1) * rows] for b in range(main)]
            even_tail = got_ref[n, h, main * rows :]
            odd_tail = got_ref[n + 1, h, main * rows :]
            even_last = jnp.concatenate(
                [even_tail, pltpu.roll(even_tail, half_lanes, 1)], axis=0
            )
            odd_last = jnp.concatenate([pltpu.roll(odd_tail, half_lanes, 1), odd_tail], axis=0)
            turned = [pltpu.roll(piece, half_lanes, 1) for piece in odd]
            blocks = list(even)
            before = even_last
            for piece in turned:
                blocks.append(jnp.where(low, before, piece))
                before = piece
            blocks.append(jnp.where(low, before, odd_last))
            for at, block in enumerate(blocks):
                lane = n * cols + at * lanes
                allowed = key_ok_ref[:, lane : lane + lanes] > 0
                out_ref[h, :, lane : lane + lanes] = jnp.where(allowed, block * log2e, far_below)
        return 0

    lax.fori_loop(0, got_ref.shape[1], one_head, 0)


def place_bias(key_ok, gathered, wide_count, rows, cols):
    narrow_count = gathered.shape[0] // wide_count
    head_count = gathered.shape[1]
    length = wide_count * rows
    return pl.pallas_call(
        functools.partial(place_bias_kernel, rows=rows, cols=cols),
        out_shape=jax.ShapeDtypeStruct((head_count, length, length), jnp.float32),
        grid=(wide_count,),
        in_specs=[
            once((1, length)),
            pl.BlockSpec((narrow_count,) + gathered.shape[1:], lambda i: (i, 0, 0, 0)),
        ],
        out_specs=pl.BlockSpec((head_count, rows, length), lambda i: (0, i, 0)),
        compiler_params=params(),
        cost_estimate=pl.CostEstimate(
            flops=gathered.size, bytes_accessed=8 * gathered.size, transcendentals=0
        ),
        name="place_bias",
    )(key_ok[None, :], gathered)


def turn_bias_kernel(key_ok_ref, got_ref, out_ref):
    queries = got_ref.shape[-1]
    plane = got_ref[:, 0, 0].reshape(-1, queries)
    allowed = key_ok_ref[...] > 0
    out_ref[0, 0] = jnp.where(allowed, plane.T * log2e, far_below)


def turn_bias(key_ok, gathered):
    devices, parts, head_count, rows, queries = gathered.shape
    length = devices * rows
    if rows % 8:
        turned = gathered.transpose(1, 2, 4, 0, 3).reshape(parts, head_count, queries, length)
        return jnp.where(key_ok > 0, turned * log2e, far_below)
    return pl.pallas_call(
        turn_bias_kernel,
        out_shape=jax.ShapeDtypeStruct((parts, head_count, queries, length), jnp.float32),
        grid=(parts, head_count),
        in_specs=[
            once((1, length)),
            pl.BlockSpec((devices, 1, 1, rows, queries), lambda p, h: (0, p, h, 0, 0)),
        ],
        out_specs=pl.BlockSpec((1, 1, queries, length), lambda p, h: (p, h, 0, 0)),
        compiler_params=pltpu.CompilerParams(vmem_limit_bytes=60 * 1024 * 1024),
        cost_estimate=pl.CostEstimate(
            flops=gathered.size, bytes_accessed=8 * gathered.size, transcendentals=0
        ),
        name="turn_bias",
    )(key_ok[None, :], gathered)


def lines_per_step(count, most):
    return max(per for per in range(1, most + 1) if count % per == 0)


def project_kernel(x_ref, w_ref, *rest, head_count, head_dim, normalise, strided):
    out_ref, scratch = (rest[-2], rest[-1]) if strided else (rest[-1], None)
    width = head_count * head_dim
    pair = 2 * width
    channels = x_ref.shape[-1]
    per = out_ref.shape[0]
    if strided:
        stride = x_ref.shape[1]

        @pl.when(pl.program_id(0) == 0)
        def _():
            scratch[...] = x_ref[...].astype(jnp.float32).reshape(scratch.shape)

    for i in range(per):
        if strided:
            at = pl.program_id(0) * per + i
            normed = scratch[pl.ds(at, x_ref.shape[0], stride=stride), :].astype(jnp.bfloat16)
        elif normalise:
            normed = layer_norm(x_ref[:, i].reshape(-1, channels).astype(jnp.float32))
        else:
            normed = x_ref[i]
        projected = jnp.dot(normed, w_ref[...], preferred_element_type=jnp.float32).astype(
            jnp.bfloat16
        )
        first = pair + width
        queries = projected[:, first : first + pair].astype(jnp.float32)
        queries = queries * (head_dim ** (-0.5) * log2e)
        upper = queries.astype(jnp.bfloat16)
        lower = (queries - upper.astype(jnp.float32)).astype(jnp.bfloat16)
        spot = lax.broadcasted_iota(jnp.int32, (1, pair), 1)
        queries = jnp.where(spot % (2 * head_dim) < head_dim, upper, lower)
        for block in range(projected.shape[1] // lanes):
            at = block * lanes
            if first <= at < first + pair:
                out_ref[i, block] = queries[:, at - first : at - first + lanes]
            else:
                out_ref[i, block] = projected[:, at : at + lanes]


def project(lines, packed, head_count, head_dim, kind, before=None, first=0, total=None):
    channels = lines.shape[-1]
    scratch = []
    if kind == "rows":
        pieces, count, cols = lines.shape[:3]
        length = pieces * cols
        per = lines_per_step(count, 2)
        spec = pl.BlockSpec((pieces, per, cols, channels), lambda i: (0, i, 0, 0))
    elif kind == "columns":
        length, count = lines.shape[:2]
        per = 1
        spec = once(lines.shape)
        scratch = [pltpu.VMEM((length * count, channels), jnp.float32)]
    else:
        count, length = lines.shape[:2]
        per = 1
        spec = pl.BlockSpec((1, length, channels), lambda i: (i, 0, 0))
    outs = packed.shape[1]
    total = count if total is None else total
    in_specs, operands, aliases = [spec, once(packed.shape)], [lines, packed], {}
    if before is not None:
        in_specs.append(pl.BlockSpec(memory_space=pl.ANY))
        operands.append(before)
        aliases = {2: 0}
    skip = first // per
    return pl.pallas_call(
        functools.partial(
            project_kernel,
            head_count=head_count,
            head_dim=head_dim,
            normalise=kind == "rows",
            strided=kind == "columns",
        ),
        out_shape=jax.ShapeDtypeStruct((total, outs // lanes, length, lanes), jnp.bfloat16),
        grid=(count // per,),
        in_specs=in_specs,
        out_specs=pl.BlockSpec((per, outs // lanes, length, lanes), lambda i: (i + skip, 0, 0, 0)),
        scratch_shapes=scratch,
        input_output_aliases=aliases,
        compiler_params=params(),
        cost_estimate=pl.CostEstimate(
            flops=2 * lines.size * outs,
            bytes_accessed=2 * lines.size * (1 + outs // channels),
            transcendentals=0,
        ),
    )(*operands)


def attend_lines(query_ref, key_ref, bias_refs, oks, head_count, head_dim):
    width = head_count * head_dim
    pair_blocks = 2 * width // lanes
    length = key_ref.shape[2]
    local = lax.broadcasted_iota(jnp.int32, (1, lanes), 1) // (2 * head_dim)
    owner = lax.broadcasted_iota(jnp.int32, (1, width), 1) // head_dim
    block_heads = lanes // (2 * head_dim)
    nothing = jnp.zeros((), jnp.bfloat16)
    jobs = [
        (i, at, h)
        for i in range(key_ref.shape[0])
        for at in range(len(bias_refs))
        for h in range(head_count)
    ]

    def score(job):
        i, at, h = job
        block = h // block_heads
        queries = query_ref[i, block, :, at].reshape(-1, lanes)
        return lax.dot_general(
            jnp.where(local == h % block_heads, queries, nothing),
            key_ref[i, block],
            (((1,), (1,)), ((), ())),
            preferred_element_type=jnp.float32,
        )

    def together(ref, i, first, *rest):
        parts = [ref[(i, first + n) + rest] for n in range(width // lanes)]
        parts = [part.reshape(-1, lanes) for part in parts]
        return parts[0] if len(parts) == 1 else jnp.concatenate(parts, axis=1)

    gated = {}
    summed = None
    coming = score(jobs[0])
    for n, (i, at, h) in enumerate(jobs):
        scores = coming
        if n + 1 < len(jobs):
            coming = score(jobs[n + 1])
        scores = scores + bias_refs[at][h].reshape(-1, length)
        top = jnp.max(scores, axis=-1, keepdims=True)
        weights = jnp.exp2(scores - top).astype(jnp.bfloat16)
        values = together(key_ref, i, pair_blocks)
        values_ones = jnp.concatenate([values, jnp.ones_like(values)], axis=1)
        both_sums = jnp.dot(weights, values_ones, preferred_element_type=jnp.float32)
        ratio = both_sums[:, :width] / both_sums[:, width:]
        summed = ratio if h == 0 else jnp.where(owner == h, ratio, summed)
        if h == head_count - 1:
            even = jnp.full((), 1.0 / length, jnp.float32).astype(jnp.bfloat16)
            total = jnp.sum(values.astype(jnp.float32), axis=0, keepdims=True)
            final = jnp.where(oks[i], summed, total * even.astype(jnp.float32))
            gates = together(query_ref, i, pair_blocks, slice(None), at).astype(jnp.float32)
            gated[i, at] = (jax.nn.sigmoid(gates) * final).astype(jnp.bfloat16)
    return gated


def out_of(gated, w_out_ref):
    return jnp.dot(gated, w_out_ref[...], preferred_element_type=jnp.float32).astype(jnp.bfloat16)


def attend_rows_kernel(
    row_ok_ref, query_ref, key_ref, bias_ref, w_out_ref, x_ref, w_bias_ref, *rest, **sizes
):
    upd_ref, next_ref, nbias_ref = rest[-3:]
    per = key_ref.shape[0]
    lines = [pl.program_id(0) * per + i for i in range(per)]
    oks = [row_ok_ref[line] > 0 for line in lines]
    gated = attend_lines(query_ref, key_ref, [bias_ref], oks, **sizes)
    for i in range(per):
        update = out_of(gated[i, 0], w_out_ref)
        upd_ref[:, i] = update.reshape(upd_ref.shape[0], *upd_ref.shape[2:])
        features = x_ref[:, i].reshape(-1, x_ref.shape[-1]).astype(jnp.float32)
        normed = layer_norm(features + update.astype(jnp.float32))
        got = lax.dot_general(
            w_bias_ref[...], normed, (((1,), (1,)), ((), ())), preferred_element_type=jnp.float32
        )
        for h in range(nbias_ref.shape[0]):
            nbias_ref[h, pl.ds(lines[i], 1), :] = got[h : h + 1]
        if len(next_ref.shape) == 4:
            devices, _, cols, channels = next_ref.shape
            narrow_count = upd_ref.shape[0]
            spread = normed.astype(jnp.float32).reshape(
                narrow_count, devices // narrow_count, cols, channels
            )
            spread = spread.transpose(1, 0, 2, 3).reshape(devices, cols, channels)
            next_ref[:, i] = spread.astype(jnp.bfloat16)
        else:
            next_ref[i] = normed


def line_specs(projected, plan, per, first, parts, skip):
    blocks, chunks, piece = plan[:3]
    total, lane_blocks, length, _ = projected.shape
    half = lane_blocks // 2
    cut = projected.reshape(total, lane_blocks, blocks, chunks, piece, lanes)
    at = first // parts
    specs = [
        pl.BlockSpec(
            (per, half, blocks, parts, piece, lanes), lambda i, ok: (i + skip, 1, 0, at, 0, 0)
        ),
        pl.BlockSpec((per, half, length, lanes), lambda i, ok: (i + skip, 0, 0, 0)),
    ]
    return specs, [cut, projected]


def attend_rows(row_ok, projected, lines, bias, w_out, w_bias_rows, chunk, before, plan):
    blocks, chunks, piece, own, wide_count = plan
    pieces, count, cols, channels = lines.shape
    length = pieces * cols
    head_count = bias.shape[0]
    width = w_out.shape[0]
    head_dim = width // head_count
    direct = own % 8 == 0
    inner = blocks // pieces
    x_cut = lines.reshape(pieces, count, inner, chunks, piece, channels)
    bias_cut = bias.reshape(head_count, blocks, chunks, piece, length)
    per = lines_per_step(count, 2)
    queries = blocks * piece
    line_block = pl.BlockSpec(
        (pieces, per, inner, None, piece, channels), lambda i, ok: (0, i, 0, chunk, 0, 0)
    )
    if direct:
        next_shape = (wide_count * pieces, count, own, channels)
        next_spec = pl.BlockSpec(
            (wide_count * pieces, per, own, channels), lambda i, ok: (0, i, 0, 0)
        )
    else:
        next_shape = (count, queries, channels)
        next_spec = pl.BlockSpec((per, queries, channels), lambda i, ok: (i, 0, 0))
    nbias_shape = (head_count, count, queries)
    scores = count * head_count * length * queries
    in_specs, operands = line_specs(projected, plan, per, chunk, 1, 0)
    in_specs += [
        pl.BlockSpec(
            (head_count, blocks, None, piece, length),
            lambda i, ok: (0, 0, chunk, 0, 0),
            pipeline_mode=pl.Buffered(1),
        ),
        once(w_out.shape),
        line_block,
        once(w_bias_rows.shape),
    ]
    operands += [bias_cut, w_out, x_cut, w_bias_rows]
    aliases = {}
    if before is not None:
        in_specs.append(pl.BlockSpec(memory_space=pl.ANY))
        operands.append(before)
        aliases = {len(operands): 0}
    upd, nxt, nbias = pl.pallas_call(
        functools.partial(attend_rows_kernel, head_count=head_count, head_dim=head_dim),
        out_shape=[
            jax.ShapeDtypeStruct(x_cut.shape, jnp.bfloat16),
            jax.ShapeDtypeStruct(next_shape, jnp.bfloat16),
            jax.ShapeDtypeStruct(nbias_shape, jnp.float32),
        ],
        grid_spec=pltpu.PrefetchScalarGridSpec(
            num_scalar_prefetch=1,
            grid=(count // per,),
            in_specs=in_specs,
            out_specs=[line_block, next_spec, pl.BlockSpec(nbias_shape, lambda i, ok: (0, 0, 0))],
        ),
        input_output_aliases=aliases,
        compiler_params=params(),
        cost_estimate=pl.CostEstimate(
            flops=4 * scores * 128, bytes_accessed=8 * lines.size, transcendentals=scores
        ),
        name="attend_rows",
    )(row_ok, *operands)
    if not direct:
        nxt = nxt.reshape(count, pieces, wide_count, own, channels).transpose(2, 1, 0, 3, 4)
        nxt = nxt.reshape(wide_count * pieces, count, own, channels)
    return upd, nxt, nbias


def attend_columns_kernel(col_ok_ref, query_ref, key_ref, *rest, parts, **sizes):
    bias_refs = [rest[0].at[at] for at in range(parts)]
    w_out_ref, out_ref = rest[1:3]
    scratch = rest[3:]
    per = key_ref.shape[0]
    blocks, piece = query_ref.shape[2], query_ref.shape[4]
    lines = [pl.program_id(0) * per + i for i in range(per)]
    oks = [col_ok_ref[line] > 0 for line in lines]
    gated = attend_lines(query_ref, key_ref, bias_refs, oks, **sizes)
    for i in range(per):
        for at in range(parts):
            update = out_of(gated[i, at], w_out_ref)
            if not scratch:
                out_ref[:, i] = update.reshape(blocks, piece, update.shape[1])
                continue
            stride = out_ref.shape[2]
            for m in range(blocks):
                first = (m * parts + at) * piece * stride + lines[i]
                scratch[0][pl.ds(first, piece, stride=stride), :] = update[
                    m * piece : (m + 1) * piece
                ].astype(jnp.float32)
    if scratch:

        @pl.when(pl.program_id(0) == pl.num_programs(0) - 1)
        def _():
            out_ref[...] = scratch[0][...].reshape(out_ref.shape).astype(jnp.bfloat16)


def attend_columns(col_ok, projected, biases, w_out, first, skip, plan):
    blocks, _, piece, own, _ = plan
    length = projected.shape[2]
    count = col_ok.shape[0]
    parts, head_count = biases.shape[:2]
    width = w_out.shape[0]
    head_dim = width // head_count
    scores = count * head_count * length * blocks * parts * piece
    per = lines_per_step(count, 2) if parts == 1 and count > own else 1
    if own % 8 == 0:
        out_shape = (blocks, parts * piece, count, width)
        out_spec = pl.BlockSpec(out_shape, lambda i, ok: (0, 0, 0, 0))
        scratch = [pltpu.VMEM((blocks * parts * piece * count, width), jnp.float32)]
    else:
        out_shape = (blocks, count, parts * piece, width)
        out_spec = pl.BlockSpec((blocks, per, parts * piece, width), lambda i, ok: (0, i, 0, 0))
        scratch = []
    in_specs, operands = line_specs(projected, plan, per, first, parts, skip // per)
    return pl.pallas_call(
        functools.partial(
            attend_columns_kernel, parts=parts, head_count=head_count, head_dim=head_dim
        ),
        out_shape=jax.ShapeDtypeStruct(out_shape, jnp.bfloat16),
        grid_spec=pltpu.PrefetchScalarGridSpec(
            num_scalar_prefetch=1,
            grid=(count // per,),
            in_specs=in_specs + [once(biases.shape), once(w_out.shape)],
            out_specs=out_spec,
            scratch_shapes=scratch,
        ),
        compiler_params=params(),
        cost_estimate=pl.CostEstimate(
            flops=4 * scores * 128, bytes_accessed=8 * count * length * width, transcendentals=scores
        ),
        name="attend_columns",
    )(col_ok, *operands, biases, w_out)


def settle_kernel(*refs, places, plan):
    _, chunks, piece, own, wide_count = plan
    tile_rows = chunks * piece
    out_ref = refs[-1]
    for j, (which, step) in enumerate(places):
        first = step * own
        for w in range(wide_count):
            inner, within = divmod(w * own, piece)
            col = inner * tile_rows + j * piece + within
            out_ref[:, col : col + own, :] = refs[which][w, :, first : first + own, :]


def settle(parts, first_row, before, places, plan, shape):
    wide_count, rows = parts[0].shape[:2]
    block = 16
    skip = first_row // block
    in_specs = [
        pl.BlockSpec((wide_count, block) + part.shape[2:], lambda i: (0, i, 0, 0))
        for part in parts
    ]
    operands, aliases = list(parts), {}
    if before is not None:
        in_specs.append(pl.BlockSpec(memory_space=pl.ANY))
        operands.append(before)
        aliases = {len(parts): 0}
    return pl.pallas_call(
        functools.partial(settle_kernel, places=places, plan=plan),
        out_shape=jax.ShapeDtypeStruct(shape, jnp.bfloat16),
        grid=(rows // block,),
        in_specs=in_specs,
        out_specs=pl.BlockSpec((block,) + shape[1:], lambda i: (i + skip, 0, 0)),
        input_output_aliases=aliases,
        compiler_params=params(),
        cost_estimate=pl.CostEstimate(
            flops=0, bytes_accessed=4 * parts[0].size * len(parts), transcendentals=0
        ),
        name="settle",
    )(*operands)


def bias_rows_of(w_bias):
    turned = w_bias.T
    return jnp.pad(turned, ((0, 16 - turned.shape[0]), (0, 0)))


def on_device(
    pair_act,
    residue_mask,
    w_proj_start,
    w_bias_start,
    w_out_start,
    w_proj_end,
    w_bias_end,
    w_out_end,
):
    wide_count = lax.axis_size("wide")
    narrow_count = lax.axis_size("narrow")
    wide_at = lax.axis_index("wide")
    narrow_at = lax.axis_index("narrow")
    tile_rows, tile_cols, channels = pair_act.shape
    head_count = w_bias_start.shape[1]
    head_dim = w_out_start.shape[0] // head_count
    length = wide_count * tile_rows
    row_count = tile_rows // narrow_count
    chunks = 1
    if tile_cols % tile_rows == 0:
        for tried in (3, 2):
            if tile_rows % (16 * tried) == 0 and tile_cols % (8 * tried * wide_count) == 0:
                chunks = tried
                break
    piece = tile_rows // chunks
    own = tile_cols // chunks // wide_count
    plan = (wide_count, chunks, piece, own, wide_count)
    key_ok = (residue_mask > 0).astype(jnp.int32)

    part = tile_bias(pair_act, bias_rows_of(w_bias_start), head_count)
    dense = tile_cols % lanes == lanes // 2 and tile_rows % 16 == 0 and narrow_count % 2 == 0
    if dense:
        part = pack_tile_bias(part)
    gathered = lax.all_gather(part, both_axes, axis=0, tiled=False)
    tile_in, part = lax.optimization_barrier((pair_act, part))
    lines = lax.all_to_all(
        tile_in.reshape(narrow_count, row_count, tile_cols, channels),
        "narrow",
        split_axis=0,
        concat_axis=0,
        tiled=True,
    )
    packed_start = pack_projection(w_proj_start, head_count, head_dim)
    projected = project(lines, packed_start, head_count, head_dim, "rows")
    if dense:
        bias = place_bias(key_ok, gathered, wide_count, tile_rows, tile_cols)
    else:
        bias = gathered.reshape(wide_count, narrow_count, head_count, tile_rows, tile_cols)
        bias = bias.transpose(2, 0, 3, 1, 4).reshape(head_count, length, length)
        bias = jnp.where(key_ok > 0, bias * log2e, far_below)

    row_ok = lax.dynamic_slice_in_dim(
        key_ok, wide_at * tile_rows + narrow_at * row_count, row_count
    )
    w_bias_rows = bias_rows_of(w_bias_end)
    order = list(range(chunks))
    soon = max(chunks - 1, 1)
    columns, waiting, next_biases = {}, [], []
    upd = None
    for step, j in enumerate(order):
        upd, nxt, nbias = attend_rows(
            row_ok, projected, lines, bias, w_out_start, w_bias_rows, j, upd, plan
        )
        waiting.append((j, nbias))
        if step in (soon - 1, chunks - 1):
            got = lax.all_gather(
                jnp.stack([nbias for _, nbias in waiting]), both_axes, axis=0, tiled=False
            )
            next_biases.append(turn_bias(key_ok, got))
            waiting = []
        got = lax.all_to_all(nxt, both_axes, split_axis=0, concat_axis=0, tiled=True)
        columns[j] = got.reshape(length, own, channels)
    mine = upd.reshape(narrow_count, row_count, tile_cols, channels)
    leaving = [
        lax.dynamic_index_in_dim(mine, (narrow_at + k) % narrow_count, 0)
        for k in range(1, narrow_count)
    ]
    leaving, mine = lax.optimization_barrier((leaving, mine))
    arrived = []
    for k in range(1, narrow_count):
        ring = [(n, (n + k) % narrow_count) for n in range(narrow_count)]
        arrived.append(lax.ppermute(leaving[k - 1], "narrow", ring))
    update_start = mine
    for k, got in enumerate(arrived, 1):
        source = (narrow_at + narrow_count - k) % narrow_count
        update_start = lax.dynamic_update_slice_in_dim(update_start, got, source, 0)
    update_start = update_start.reshape(tile_rows, tile_cols, channels)

    packed_end = pack_projection(w_proj_end, head_count, head_dim)
    projected_end, col_ok = {}, []
    home_of = [(0, step) if step < soon else (soon, step - soon) for step in range(chunks)]
    for step, j in enumerate(order):
        group, place = home_of[step]
        lines_end = columns[j]
        if own % 8:
            lines_end = lines_end.transpose(1, 0, 2)
        projected_end[group] = project(
            lines_end,
            packed_end,
            head_count,
            head_dim,
            "plain" if own % 8 else "columns",
            projected_end.get(group),
            place * own,
            (soon if group == 0 else chunks - soon) * own,
        )
        at = wide_at * own + jnp.arange(own)
        at = narrow_at * tile_cols + at // piece * tile_rows + j * piece + at % piece
        col_ok.append(key_ok[at])

    def columns_of(step, count, first):
        return attend_columns(
            jnp.concatenate(col_ok[step : step + count]),
            projected_end[home_of[step][0]],
            next_biases[0 if first == 0 else 1],
            w_out_end,
            first,
            home_of[step][1] * own,
            plan,
        )

    parts = []
    for step in range(chunks):
        got = columns_of(step, 1, 0)
        parts.append(lax.all_to_all(got, "wide", split_axis=0, concat_axis=0, tiled=True))
    if chunks == 1:
        if own % 8:
            parts[0] = parts[0].transpose(0, 2, 1, 3)
        return (update_start, parts[0].transpose(1, 0, 2, 3).reshape(pair_act.shape))
    late = []
    for step, count in ((0, soon), (soon, chunks - soon)):
        got = columns_of(step, count, soon)
        late.append(lax.all_to_all(got, "wide", split_axis=0, concat_axis=0, tiled=True))
    settled = settle(parts, 0, None, [(n, 0) for n in order], plan, pair_act.shape)
    places = [(0, n) for n in range(soon)] + [(1, n) for n in range(chunks - soon)]
    return (update_start, settle(late, soon * piece, settled, places, plan, pair_act.shape))


def solution(mesh):
    in_specs = (P("wide", "narrow", None), P(), P(), P(), P(), P(), P(), P())
    out_specs = (P("wide", "narrow", None), P("wide", "narrow", None))
    return jax.shard_map(
        on_device, mesh=mesh, in_specs=in_specs, out_specs=out_specs, check_vma=False
    )
```

```python
import functools

import jax
import jax.numpy as jnp
from jax import lax
from jax.experimental import pallas as pl
from jax.experimental.pallas import tpu as pltpu
from jax.sharding import PartitionSpec as P


norm_eps = 1e-05
log2e = 1.4426950408889634
far_below = -1e30
safe_product = 50.0
lanes = 128
both_axes = ("wide", "narrow")


def params(megabytes=60):
    return pltpu.CompilerParams(
        dimension_semantics=("arbitrary",), vmem_limit_bytes=megabytes * 1024 * 1024
    )


def once(shape):
    return pl.BlockSpec(
        shape, lambda *_: (0,) * len(shape), pipeline_mode=pl.Buffered(1)
    )


def layer_norm(features):
    average = jnp.mean(features, axis=-1, keepdims=True)
    centred = features - average
    spread = jnp.mean(centred * centred, axis=-1, keepdims=True)
    return (centred * lax.rsqrt(spread + norm_eps)).astype(jnp.bfloat16)


def masked_bias(bias, allowed):
    bias = jnp.where(allowed, bias * log2e, far_below)
    return bias - jnp.max(bias, axis=-1, keepdims=True)


def pack_projection(w_proj, head_count, head_dim):
    split = w_proj.reshape(w_proj.shape[0], head_count, 4, head_dim)
    twice = jnp.concatenate([split, split], axis=-1)
    parts = [twice[:, :, 1], split[:, :, 2], twice[:, :, 0], split[:, :, 3]]
    return jnp.concatenate([part.reshape(w_proj.shape[0], -1) for part in parts], axis=1)


def tile_bias_kernel(x_ref, w_ref, out_ref, *, head_count):
    for i in range(x_ref.shape[0]):
        normed = layer_norm(x_ref[i].astype(jnp.float32))
        got = lax.dot_general(
            w_ref[...], normed, (((1,), (1,)), ((), ())), preferred_element_type=jnp.float32
        )
        for h in range(head_count):
            out_ref[h, i : i + 1, :] = got[h : h + 1]


def tile_bias(tile, w_bias_rows, head_count):
    rows, cols, channels = tile.shape
    block = 8 if rows % 8 == 0 else rows
    return pl.pallas_call(
        functools.partial(tile_bias_kernel, head_count=head_count),
        out_shape=jax.ShapeDtypeStruct((head_count, rows, cols), jnp.float32),
        grid=(rows // block,),
        in_specs=[
            pl.BlockSpec((block, cols, channels), lambda i: (i, 0, 0)),
            once(w_bias_rows.shape),
        ],
        out_specs=pl.BlockSpec((head_count, block, cols), lambda i: (0, i, 0)),
        compiler_params=params(16),
        cost_estimate=pl.CostEstimate(
            flops=32 * tile.size, bytes_accessed=2 * tile.size, transcendentals=0
        ),
        name="tile_bias",
    )(tile, w_bias_rows)


def pack_tile_bias(part):
    rows, cols = part.shape[1:]
    main = cols // lanes * lanes
    left, right = part[:, :, :main], part[:, :, main:]
    half = rows // 2
    tail = jnp.concatenate([right[:, :half], right[:, half:]], axis=2)
    split = [left[:, :, at : at + lanes] for at in range(0, main, lanes)]
    return jnp.concatenate(split + [tail], axis=1)


def place_bias_kernel(key_ok_ref, got_ref, out_ref, *, rows, cols):
    main = cols // lanes
    half_lanes = lanes // 2
    low = lax.broadcasted_iota(jnp.int32, (1, lanes), 1) < half_lanes

    def one_head(h, _):
        placed = []
        for n in range(0, got_ref.shape[0], 2):
            even = [got_ref[n, h, b * rows : (b + 1) * rows] for b in range(main)]
            odd = [got_ref[n + 1, h, b * rows : (b + 1) * rows] for b in range(main)]
            even_tail = got_ref[n, h, main * rows :]
            odd_tail = got_ref[n + 1, h, main * rows :]
            even_last = jnp.concatenate(
                [even_tail, pltpu.roll(even_tail, half_lanes, 1)], axis=0
            )
            odd_last = jnp.concatenate([pltpu.roll(odd_tail, half_lanes, 1), odd_tail], axis=0)
            turned = [pltpu.roll(piece, half_lanes, 1) for piece in odd]
            blocks = list(even)
            before = even_last
            for piece in turned:
                blocks.append(jnp.where(low, before, piece))
                before = piece
            blocks.append(jnp.where(low, before, odd_last))
            for at, block in enumerate(blocks):
                lane = n * cols + at * lanes
                allowed = key_ok_ref[:, lane : lane + lanes] > 0
                placed.append((lane, jnp.where(allowed, block * log2e, far_below)))
        top = functools.reduce(jnp.maximum, [block for _, block in placed])
        top = jnp.max(top, axis=-1, keepdims=True)
        for lane, block in placed:
            out_ref[h, :, lane : lane + lanes] = block - top
        return 0

    lax.fori_loop(0, got_ref.shape[1], one_head, 0)


def place_bias(key_ok, gathered, wide_count, rows, cols):
    narrow_count = gathered.shape[0] // wide_count
    head_count = gathered.shape[1]
    length = wide_count * rows
    return pl.pallas_call(
        functools.partial(place_bias_kernel, rows=rows, cols=cols),
        out_shape=jax.ShapeDtypeStruct((head_count, length, length), jnp.float32),
        grid=(wide_count,),
        in_specs=[
            once((1, length)),
            pl.BlockSpec((narrow_count,) + gathered.shape[1:], lambda i: (i, 0, 0, 0)),
        ],
        out_specs=pl.BlockSpec((head_count, rows, length), lambda i: (0, i, 0)),
        compiler_params=params(16),
        cost_estimate=pl.CostEstimate(
            flops=gathered.size, bytes_accessed=8 * gathered.size, transcendentals=0
        ),
        name="place_bias",
    )(key_ok[None, :], gathered)


def turn_bias_kernel(key_ok_ref, got_ref, out_ref):
    queries = got_ref.shape[-1]
    plane = got_ref[:, 0, 0].reshape(-1, queries)
    allowed = key_ok_ref[...] > 0
    out_ref[0] = masked_bias(plane.T, allowed)


def turn_bias(key_ok, gathered, part):
    devices, _, head_count, rows, queries = gathered.shape
    length = devices * rows
    return pl.pallas_call(
        turn_bias_kernel,
        out_shape=jax.ShapeDtypeStruct((head_count, queries, length), jnp.float32),
        grid=(head_count,),
        in_specs=[
            once((1, length)),
            pl.BlockSpec((devices, 1, 1, rows, queries), lambda h: (0, part, h, 0, 0)),
        ],
        out_specs=pl.BlockSpec((1, queries, length), lambda h: (h, 0, 0)),
        compiler_params=params(),
        cost_estimate=pl.CostEstimate(
            flops=gathered.size, bytes_accessed=8 * gathered.size, transcendentals=0
        ),
        name="turn_bias",
    )(key_ok[None, :], gathered)


def lines_per_step(count, most):
    return max(per for per in range(1, most + 1) if count % per == 0)


def project_kernel(x_ref, w_ref, *rest, head_count, head_dim, normalise, strided):
    (*rest, scratch) = rest if strided else (*rest, None)
    sum_ref, (out_ref, norm_ref) = rest[0], rest[-2:]
    width = head_count * head_dim
    pair = 2 * width
    channels = x_ref.shape[-1]
    per = out_ref.shape[0]
    if strided:
        stride = x_ref.shape[1]

        @pl.when(pl.program_id(0) == 0)
        def _():
            scratch[...] = x_ref[...].astype(jnp.float32).reshape(scratch.shape)

    for i in range(per):
        if strided:
            at = pl.program_id(0) * per + i
            normed = scratch[pl.ds(at, x_ref.shape[0], stride=stride), :].astype(jnp.bfloat16)
        elif normalise:
            normed = layer_norm(x_ref[:, i].reshape(-1, channels).astype(jnp.float32))
        else:
            normed = x_ref[i]
        projected = jnp.dot(normed, w_ref[...], preferred_element_type=jnp.float32).astype(
            jnp.bfloat16
        )
        first = pair + width
        queries = projected[:, first : first + pair].astype(jnp.float32)
        queries = queries * (head_dim ** (-0.5) * log2e)
        upper = queries.astype(jnp.bfloat16)
        lower = (queries - upper.astype(jnp.float32)).astype(jnp.bfloat16)
        spot = lax.broadcasted_iota(jnp.int32, (1, pair), 1)
        queries = jnp.where(spot % (2 * head_dim) < head_dim, upper, lower)
        for spot, part in enumerate((queries, projected[:, :pair])):
            squares = part.astype(jnp.float32)
            squares = (squares * squares).astype(jnp.bfloat16)
            sums = jnp.dot(squares, sum_ref[...], preferred_element_type=jnp.float32)
            norm_ref[i, spot : spot + 1, :] = jnp.max(sums, axis=0, keepdims=True)
        for block in range(projected.shape[1] // lanes):
            at = block * lanes
            if first <= at < first + pair:
                out_ref[i, block] = queries[:, at - first : at - first + lanes]
            else:
                out_ref[i, block] = projected[:, at : at + lanes]


def project(lines, packed, head_count, head_dim, kind, before=None, first=0, total=None):
    channels = lines.shape[-1]
    scratch = []
    if kind == "rows":
        pieces, count, cols = lines.shape[:3]
        length = pieces * cols
        per = lines_per_step(count, 2)
        spec = pl.BlockSpec((pieces, per, cols, channels), lambda i: (0, i, 0, 0))
    elif kind == "columns":
        length, count = lines.shape[:2]
        per = 1
        spec = once(lines.shape)
        scratch = [pltpu.VMEM((length * count, channels), jnp.float32)]
    else:
        count, length = lines.shape[:2]
        per = 1
        spec = pl.BlockSpec((1, length, channels), lambda i: (i, 0, 0))
    outs = packed.shape[1]
    total = count if total is None else total
    pair = 2 * head_count * head_dim
    owner = jnp.arange(pair)[:, None] // (2 * head_dim)
    sums = (owner == jnp.arange(lanes)[None, :]).astype(jnp.bfloat16)
    in_specs = [spec, once(packed.shape), once(sums.shape)]
    operands, aliases = [lines, packed, sums], {}
    if before is not None:
        in_specs.append(pl.BlockSpec(memory_space=pl.ANY))
        operands.append(before)
        aliases = {3: 0}
    skip = first // per
    out, norms = pl.pallas_call(
        functools.partial(
            project_kernel,
            head_count=head_count,
            head_dim=head_dim,
            normalise=kind == "rows",
            strided=kind == "columns",
        ),
        out_shape=[
            jax.ShapeDtypeStruct((total, outs // lanes, length, lanes), jnp.bfloat16),
            jax.ShapeDtypeStruct((count, 8, lanes), jnp.float32),
        ],
        grid=(count // per,),
        in_specs=in_specs,
        out_specs=[
            pl.BlockSpec((per, outs // lanes, length, lanes), lambda i: (i + skip, 0, 0, 0)),
            pl.BlockSpec((per, 8, lanes), lambda i: (i, 0, 0)),
        ],
        scratch_shapes=scratch,
        input_output_aliases=aliases,
        compiler_params=params(),
        cost_estimate=pl.CostEstimate(
            flops=2 * lines.size * outs,
            bytes_accessed=2 * lines.size * (1 + outs // channels),
            transcendentals=0,
        ),
    )(*operands)
    most = jnp.max(norms[:, 0, :head_count] * norms[:, 1, :head_count], axis=-1) / 2
    return out, (most * 1.1 < safe_product**2).astype(jnp.int32)


def attend_lines(query_ref, key_ref, bias_refs, oks, bounded, head_count, head_dim):
    width = head_count * head_dim
    pair_blocks = 2 * width // lanes
    length = key_ref.shape[2]
    local = lax.broadcasted_iota(jnp.int32, (1, lanes), 1) // (2 * head_dim)
    owner = lax.broadcasted_iota(jnp.int32, (1, width), 1) // head_dim
    block_heads = lanes // (2 * head_dim)
    nothing = jnp.zeros((), jnp.bfloat16)

    def together(ref, i, first, *rest):
        parts = [ref[(i, first + n) + rest] for n in range(width // lanes)]
        parts = [part.reshape(-1, lanes) for part in parts]
        return parts[0] if len(parts) == 1 else jnp.concatenate(parts, axis=1)

    def score(i, at, h):
        block = h // block_heads
        queries = query_ref[i, block, :, at].reshape(-1, lanes)
        return lax.dot_general(
            jnp.where(local == h % block_heads, queries, nothing),
            key_ref[i, block],
            (((1,), (1,)), ((), ())),
            preferred_element_type=jnp.float32,
        )

    def head_sums(i, at, h, scores):
        scores = scores + bias_refs[at][h].reshape(-1, length)
        if not bounded:
            scores = scores - jnp.max(scores, axis=-1, keepdims=True)
        weights = jnp.exp2(scores).astype(jnp.bfloat16)
        values = together(key_ref, i, pair_blocks)
        values_ones = jnp.concatenate([values, jnp.ones_like(values)], axis=1)
        both_sums = jnp.dot(weights, values_ones, preferred_element_type=jnp.float32)
        return both_sums[:, :width] / both_sums[:, width:]

    def finish(i, at, summed):
        even = jnp.full((), 1.0 / length, jnp.float32).astype(jnp.bfloat16)
        values = together(key_ref, i, pair_blocks)
        total = jnp.sum(values.astype(jnp.float32), axis=0, keepdims=True)
        final = jnp.where(oks[i], summed, total * even.astype(jnp.float32))
        gates = together(query_ref, i, pair_blocks, slice(None), at).astype(jnp.float32)
        return (jax.nn.sigmoid(gates) * final).astype(jnp.bfloat16)

    spots = [(i, at) for i in range(key_ref.shape[0]) for at in range(len(bias_refs))]
    gated = {}
    if not bounded:
        queries = query_ref.shape[2] * query_ref.shape[4]
        for i, at in spots:

            def one_head(h, summed):
                return jnp.where(owner == h, head_sums(i, at, h, score(i, at, h)), summed)

            start = jnp.zeros((queries, width), jnp.float32)
            gated[i, at] = finish(i, at, lax.fori_loop(0, head_count, one_head, start))
        return gated

    jobs = [(i, at, h) for i, at in spots for h in range(head_count)]
    coming = score(*jobs[0])
    summed = None
    for n, (i, at, h) in enumerate(jobs):
        scores = coming
        if n + 1 < len(jobs):
            coming = score(*jobs[n + 1])
        ratio = head_sums(i, at, h, scores)
        summed = ratio if h == 0 else jnp.where(owner == h, ratio, summed)
        if h == head_count - 1:
            gated[i, at] = finish(i, at, summed)
    return gated


def either_way(bounded_ref, lines, run):
    bounded = functools.reduce(jnp.minimum, [bounded_ref[line] for line in lines]) > 0
    pl.when(bounded)(lambda: run(True))
    pl.when(jnp.logical_not(bounded))(lambda: run(False))


def out_of(gated, w_out_ref):
    return jnp.dot(gated, w_out_ref[...], preferred_element_type=jnp.float32).astype(jnp.bfloat16)


def attend_rows_kernel(
    row_ok_ref, bounded_ref, query_ref, key_ref, bias_ref, w_out_ref, x_ref, w_bias_ref, *rest, **sizes
):
    upd_ref, next_ref, nbias_ref = rest[-3:]
    per = key_ref.shape[0]
    lines = [pl.program_id(0) * per + i for i in range(per)]
    oks = [row_ok_ref[line] > 0 for line in lines]

    def run(bounded):
        gated = attend_lines(query_ref, key_ref, [bias_ref], oks, bounded, **sizes)
        for i in range(per):
            update = out_of(gated[i, 0], w_out_ref)
            upd_ref[:, i] = update.reshape(upd_ref.shape[0], *upd_ref.shape[2:])
            features = x_ref[:, i].reshape(-1, x_ref.shape[-1]).astype(jnp.float32)
            normed = layer_norm(features + update.astype(jnp.float32))
            got = lax.dot_general(
                w_bias_ref[...], normed, (((1,), (1,)), ((), ())), preferred_element_type=jnp.float32
            )
            for h in range(nbias_ref.shape[0]):
                nbias_ref[h, pl.ds(lines[i], 1), :] = got[h : h + 1]
            if len(next_ref.shape) == 4:
                devices, _, cols, channels = next_ref.shape
                narrow_count = upd_ref.shape[0]
                spread = normed.astype(jnp.float32).reshape(
                    narrow_count, devices // narrow_count, cols, channels
                )
                spread = spread.transpose(1, 0, 2, 3).reshape(devices, cols, channels)
                next_ref[:, i] = spread.astype(jnp.bfloat16)
            else:
                next_ref[i] = normed

    either_way(bounded_ref, lines, run)


def line_specs(projected, plan, per, first, parts, skip):
    blocks, chunks, piece = plan[:3]
    total, lane_blocks, length, _ = projected.shape
    half = lane_blocks // 2
    cut = projected.reshape(total, lane_blocks, blocks, chunks, piece, lanes)
    at = first // parts
    specs = [
        pl.BlockSpec(
            (per, half, blocks, parts, piece, lanes), lambda i, *_: (i + skip, 1, 0, at, 0, 0)
        ),
        pl.BlockSpec((per, half, length, lanes), lambda i, *_: (i + skip, 0, 0, 0)),
    ]
    return specs, [cut, projected]


def attend_rows(row_ok, bounded, projected, lines, bias, w_out, w_bias_rows, chunk, before, plan):
    blocks, chunks, piece, own, wide_count = plan
    pieces, count, cols, channels = lines.shape
    length = pieces * cols
    head_count = bias.shape[0]
    width = w_out.shape[0]
    head_dim = width // head_count
    direct = own % 8 == 0
    inner = blocks // pieces
    x_cut = lines.reshape(pieces, count, inner, chunks, piece, channels)
    bias_cut = bias.reshape(head_count, blocks, chunks, piece, length)
    per = lines_per_step(count, 2)
    queries = blocks * piece
    line_block = pl.BlockSpec(
        (pieces, per, inner, None, piece, channels), lambda i, *_: (0, i, 0, chunk, 0, 0)
    )
    if direct:
        next_shape = (wide_count * pieces, count, own, channels)
        next_spec = pl.BlockSpec(
            (wide_count * pieces, per, own, channels), lambda i, *_: (0, i, 0, 0)
        )
    else:
        next_shape = (count, queries, channels)
        next_spec = pl.BlockSpec((per, queries, channels), lambda i, *_: (i, 0, 0))
    nbias_shape = (head_count, count, queries)
    scores = count * head_count * length * queries
    in_specs, operands = line_specs(projected, plan, per, chunk, 1, 0)
    in_specs += [
        pl.BlockSpec(
            (head_count, blocks, None, piece, length),
            lambda i, *_: (0, 0, chunk, 0, 0),
            pipeline_mode=pl.Buffered(1),
        ),
        once(w_out.shape),
        line_block,
        once(w_bias_rows.shape),
    ]
    operands += [bias_cut, w_out, x_cut, w_bias_rows]
    aliases = {}
    if before is not None:
        in_specs.append(pl.BlockSpec(memory_space=pl.ANY))
        operands.append(before)
        aliases = {len(operands) + 1: 0}
    upd, nxt, nbias = pl.pallas_call(
        functools.partial(attend_rows_kernel, head_count=head_count, head_dim=head_dim),
        out_shape=[
            jax.ShapeDtypeStruct(x_cut.shape, jnp.bfloat16),
            jax.ShapeDtypeStruct(next_shape, jnp.bfloat16),
            jax.ShapeDtypeStruct(nbias_shape, jnp.float32),
        ],
        grid_spec=pltpu.PrefetchScalarGridSpec(
            num_scalar_prefetch=2,
            grid=(count // per,),
            in_specs=in_specs,
            out_specs=[line_block, next_spec, pl.BlockSpec(nbias_shape, lambda i, *_: (0, 0, 0))],
        ),
        input_output_aliases=aliases,
        compiler_params=params(),
        cost_estimate=pl.CostEstimate(
            flops=4 * scores * 128, bytes_accessed=8 * lines.size, transcendentals=scores
        ),
        name="attend_rows",
    )(row_ok, bounded, *operands)
    if not direct:
        nxt = nxt.reshape(count, pieces, wide_count, own, channels).transpose(2, 1, 0, 3, 4)
        nxt = nxt.reshape(wide_count * pieces, count, own, channels)
    return upd, nxt, nbias


def attend_columns_kernel(col_ok_ref, bounded_ref, query_ref, key_ref, *rest, parts, **sizes):
    bias_refs, w_out_ref, out_ref = rest[:parts], rest[parts], rest[parts + 1]
    scratch = rest[parts + 2 :]
    per = key_ref.shape[0]
    blocks, piece = query_ref.shape[2], query_ref.shape[4]
    lines = [pl.program_id(0) * per + i for i in range(per)]
    oks = [col_ok_ref[line] > 0 for line in lines]

    def run(bounded):
        gated = attend_lines(query_ref, key_ref, bias_refs, oks, bounded, **sizes)
        for i in range(per):
            for at in range(parts):
                update = out_of(gated[i, at], w_out_ref)
                if not scratch:
                    out_ref[:, i] = update.reshape(blocks, piece, update.shape[1])
                    continue
                stride = out_ref.shape[2]
                for m in range(blocks):
                    first = (m * parts + at) * piece * stride + lines[i]
                    scratch[0][pl.ds(first, piece, stride=stride), :] = update[
                        m * piece : (m + 1) * piece
                    ].astype(jnp.float32)

    either_way(bounded_ref, lines, run)
    if scratch:

        @pl.when(pl.program_id(0) == pl.num_programs(0) - 1)
        def _():
            out_ref[...] = scratch[0][...].reshape(out_ref.shape).astype(jnp.bfloat16)


def attend_columns(col_ok, bounded, projected, biases, w_out, first, skip, plan):
    blocks, _, piece, own, _ = plan
    length = projected.shape[2]
    count = col_ok.shape[0]
    parts = len(biases)
    head_count = biases[0].shape[0]
    width = w_out.shape[0]
    head_dim = width // head_count
    scores = count * head_count * length * blocks * parts * piece
    per = lines_per_step(count, 2) if parts == 1 else 1
    if own % 8 == 0:
        out_shape = (blocks, parts * piece, count, width)
        out_spec = pl.BlockSpec(out_shape, lambda i, *_: (0, 0, 0, 0))
        scratch = [pltpu.VMEM((blocks * parts * piece * count, width), jnp.float32)]
    else:
        out_shape = (blocks, count, parts * piece, width)
        out_spec = pl.BlockSpec((blocks, per, parts * piece, width), lambda i, *_: (0, i, 0, 0))
        scratch = []
    in_specs, operands = line_specs(projected, plan, per, first, parts, skip // per)
    return pl.pallas_call(
        functools.partial(
            attend_columns_kernel, parts=parts, head_count=head_count, head_dim=head_dim
        ),
        out_shape=jax.ShapeDtypeStruct(out_shape, jnp.bfloat16),
        grid_spec=pltpu.PrefetchScalarGridSpec(
            num_scalar_prefetch=2,
            grid=(count // per,),
            in_specs=in_specs + [once(biases[0].shape)] * parts + [once(w_out.shape)],
            out_specs=out_spec,
            scratch_shapes=scratch,
        ),
        compiler_params=params(),
        cost_estimate=pl.CostEstimate(
            flops=4 * scores * 128, bytes_accessed=8 * count * length * width, transcendentals=scores
        ),
        name="attend_columns",
    )(col_ok, bounded, *operands, *biases, w_out)


def settle_kernel(*refs, order, plan):
    _, chunks, piece, own, wide_count = plan
    tile_rows = chunks * piece
    out_ref = refs[-1]
    for step, j in enumerate(order):
        ref, first = (refs[0], step * own) if len(refs) < chunks else (refs[step], 0)
        for w in range(wide_count):
            inner, within = divmod(w * own, piece)
            col = inner * tile_rows + j * piece + within
            out_ref[:, col : col + own, :] = ref[w, :, first : first + own, :]


def settle(parts, first_row, before, order, plan, shape):
    wide_count, rows, _, _ = parts[0].shape
    block = 16
    skip = first_row // block
    in_specs = [
        pl.BlockSpec((wide_count, block) + part.shape[2:], lambda i: (0, i, 0, 0))
        for part in parts
    ]
    operands, aliases = list(parts), {}
    if before is not None:
        in_specs.append(pl.BlockSpec(memory_space=pl.ANY))
        operands.append(before)
        aliases = {len(parts): 0}
    return pl.pallas_call(
        functools.partial(settle_kernel, order=order, plan=plan),
        out_shape=jax.ShapeDtypeStruct(shape, jnp.bfloat16),
        grid=(rows // block,),
        in_specs=in_specs,
        out_specs=pl.BlockSpec((block,) + shape[1:], lambda i: (i + skip, 0, 0)),
        input_output_aliases=aliases,
        compiler_params=params(),
        cost_estimate=pl.CostEstimate(
            flops=0, bytes_accessed=4 * parts[0].size * len(parts), transcendentals=0
        ),
        name="settle",
    )(*operands)


def bias_rows_of(w_bias):
    turned = w_bias.T
    return jnp.pad(turned, ((0, 16 - turned.shape[0]), (0, 0)))


def on_device(
    pair_act,
    residue_mask,
    w_proj_start,
    w_bias_start,
    w_out_start,
    w_proj_end,
    w_bias_end,
    w_out_end,
):
    wide_count = lax.axis_size("wide")
    narrow_count = lax.axis_size("narrow")
    wide_at = lax.axis_index("wide")
    narrow_at = lax.axis_index("narrow")
    tile_rows, tile_cols, channels = pair_act.shape
    head_count = w_bias_start.shape[1]
    head_dim = w_out_start.shape[0] // head_count
    length = wide_count * tile_rows
    row_count = tile_rows // narrow_count
    chunks = 1
    if tile_cols % tile_rows == 0:
        for tried in (3, 2):
            if tile_rows % (16 * tried) == 0 and tile_cols % (8 * tried * wide_count) == 0:
                chunks = tried
                break
    piece = tile_rows // chunks
    own = tile_cols // chunks // wide_count
    plan = (wide_count, chunks, piece, own, wide_count)
    key_ok = (residue_mask > 0).astype(jnp.int32)

    part = tile_bias(pair_act, bias_rows_of(w_bias_start), head_count)
    dense = tile_cols % lanes == lanes // 2 and tile_rows % 16 == 0 and narrow_count % 2 == 0
    if dense:
        part = pack_tile_bias(part)
    gathered = lax.all_gather(part, both_axes, axis=0, tiled=False)
    tile_in, part = lax.optimization_barrier((pair_act, part))
    lines = lax.all_to_all(
        tile_in.reshape(narrow_count, row_count, tile_cols, channels),
        "narrow",
        split_axis=0,
        concat_axis=0,
        tiled=True,
    )
    packed_start = pack_projection(w_proj_start, head_count, head_dim)
    projected, bounded = project(lines, packed_start, head_count, head_dim, "rows")
    if dense:
        bias = place_bias(key_ok, gathered, wide_count, tile_rows, tile_cols)
    else:
        bias = gathered.reshape(wide_count, narrow_count, head_count, tile_rows, tile_cols)
        bias = bias.transpose(2, 0, 3, 1, 4).reshape(head_count, length, length)
        bias = masked_bias(bias, key_ok > 0)

    row_ok = lax.dynamic_slice_in_dim(
        key_ok, wide_at * tile_rows + narrow_at * row_count, row_count
    )
    w_bias_rows = bias_rows_of(w_bias_end)
    order = [chunks - 1] + list(range(chunks - 1))
    columns, waiting, next_biases = {}, [], {}
    upd = None
    for step, j in enumerate(order):
        upd, nxt, nbias = attend_rows(
            row_ok, bounded, projected, lines, bias, w_out_start, w_bias_rows, j, upd, plan
        )
        waiting.append((j, nbias))
        if step in (0, chunks - 1):
            got = lax.all_gather(
                jnp.stack([nbias for _, nbias in waiting]), both_axes, axis=0, tiled=False
            )
            for n, (k, _) in enumerate(waiting):
                if row_count % 8 == 0:
                    turned = turn_bias(key_ok, got, n)
                else:
                    turned = got[:, n].transpose(1, 3, 0, 2).reshape(head_count, -1, length)
                    turned = masked_bias(turned, key_ok > 0)
                next_biases[k] = turned
            waiting = []
        got = lax.all_to_all(nxt, both_axes, split_axis=0, concat_axis=0, tiled=True)
        columns[j] = got.reshape(length, own, channels)
    mine = upd.reshape(narrow_count, row_count, tile_cols, channels)
    leaving = [
        lax.dynamic_index_in_dim(mine, (narrow_at + k) % narrow_count, 0)
        for k in range(1, narrow_count)
    ]
    leaving, mine = lax.optimization_barrier((leaving, mine))
    arrived = []
    for k in range(1, narrow_count):
        ring = [(n, (n + k) % narrow_count) for n in range(narrow_count)]
        arrived.append(lax.ppermute(leaving[k - 1], "narrow", ring))
    update_start = mine
    for k, got in enumerate(arrived, 1):
        source = (narrow_at + narrow_count - k) % narrow_count
        update_start = lax.dynamic_update_slice_in_dim(update_start, got, source, 0)
    update_start = update_start.reshape(tile_rows, tile_cols, channels)

    packed_end = pack_projection(w_proj_end, head_count, head_dim)
    projected_end, col_ok, bounded_end = None, [], []
    for step, j in enumerate(order):
        lines_end = columns[j]
        if own % 8:
            lines_end = lines_end.transpose(1, 0, 2)
        projected_end, bounded = project(
            lines_end,
            packed_end,
            head_count,
            head_dim,
            "plain" if own % 8 else "columns",
            projected_end,
            step * own,
            chunks * own,
        )
        at = wide_at * own + jnp.arange(own)
        at = narrow_at * tile_cols + at // piece * tile_rows + j * piece + at % piece
        col_ok.append(key_ok[at])
        bounded_end.append(bounded)

    got = attend_columns(
        jnp.concatenate(col_ok),
        jnp.concatenate(bounded_end),
        projected_end,
        [next_biases[order[0]]],
        w_out_end,
        order[0],
        0,
        plan,
    )
    got = lax.all_to_all(got, "wide", split_axis=0, concat_axis=0, tiled=True)
    if chunks == 1:
        return (update_start, got.transpose(2, 0, 1, 3).reshape(pair_act.shape))
    settled = settle([got], (chunks - 1) * piece, None, order, plan, pair_act.shape)
    late = []
    for step, j in enumerate(order):
        got = attend_columns(
            col_ok[step],
            bounded_end[step],
            projected_end,
            [next_biases[k] for k in range(chunks - 1)],
            w_out_end,
            0,
            step * own,
            plan,
        )
        late.append(lax.all_to_all(got, "wide", split_axis=0, concat_axis=0, tiled=True))
    return (update_start, settle(late, 0, settled, order, plan, pair_act.shape))


def solution(mesh):
    in_specs = (P("wide", "narrow", None), P(), P(), P(), P(), P(), P(), P())
    out_specs = (P("wide", "narrow", None), P("wide", "narrow", None))
    return jax.shard_map(
        on_device, mesh=mesh, in_specs=in_specs, out_specs=out_specs, check_vma=False
    )
```

```python
import functools

import jax
import jax.numpy as jnp
from jax import lax
from jax.experimental import pallas as pl
from jax.experimental.pallas import tpu as pltpu
from jax.sharding import PartitionSpec as P


norm_eps = 1e-05
log2e = 1.4426950408889634
far_below = -1e30
safe_product = 50.0
lanes = 128
both_axes = ("wide", "narrow")


def params(megabytes=60):
    return pltpu.CompilerParams(
        dimension_semantics=("arbitrary",), vmem_limit_bytes=megabytes * 1024 * 1024
    )


def once(shape):
    return pl.BlockSpec(
        shape, lambda *_: (0,) * len(shape), pipeline_mode=pl.Buffered(1)
    )


def layer_norm(features):
    average = jnp.mean(features, axis=-1, keepdims=True)
    centred = features - average
    spread = jnp.mean(centred * centred, axis=-1, keepdims=True)
    return (centred * lax.rsqrt(spread + norm_eps)).astype(jnp.bfloat16)


def masked_bias(bias, allowed):
    bias = jnp.where(allowed, bias * log2e, far_below)
    return bias - jnp.max(bias, axis=-1, keepdims=True)


def pack_projection(w_proj, head_count, head_dim):
    split = w_proj.reshape(w_proj.shape[0], head_count, 4, head_dim)
    twice = jnp.concatenate([split, split], axis=-1)
    parts = [twice[:, :, 1], split[:, :, 2], twice[:, :, 0], split[:, :, 3]]
    return jnp.concatenate([part.reshape(w_proj.shape[0], -1) for part in parts], axis=1)


def tile_bias_kernel(x_ref, w_ref, out_ref, *, head_count):
    for i in range(x_ref.shape[0]):
        normed = layer_norm(x_ref[i].astype(jnp.float32))
        got = lax.dot_general(
            w_ref[...], normed, (((1,), (1,)), ((), ())), preferred_element_type=jnp.float32
        )
        for h in range(head_count):
            out_ref[h, i : i + 1, :] = got[h : h + 1]


def tile_bias(tile, w_bias_rows, head_count):
    rows, cols, channels = tile.shape
    block = 8 if rows % 8 == 0 else rows
    return pl.pallas_call(
        functools.partial(tile_bias_kernel, head_count=head_count),
        out_shape=jax.ShapeDtypeStruct((head_count, rows, cols), jnp.float32),
        grid=(rows // block,),
        in_specs=[
            pl.BlockSpec((block, cols, channels), lambda i: (i, 0, 0)),
            once(w_bias_rows.shape),
        ],
        out_specs=pl.BlockSpec((head_count, block, cols), lambda i: (0, i, 0)),
        compiler_params=params(16),
        cost_estimate=pl.CostEstimate(
            flops=32 * tile.size, bytes_accessed=2 * tile.size, transcendentals=0
        ),
        name="tile_bias",
    )(tile, w_bias_rows)


def pack_tile_bias(part):
    rows, cols = part.shape[1:]
    main = cols // lanes * lanes
    left, right = part[:, :, :main], part[:, :, main:]
    half = rows // 2
    tail = jnp.concatenate([right[:, :half], right[:, half:]], axis=2)
    split = [left[:, :, at : at + lanes] for at in range(0, main, lanes)]
    return jnp.concatenate(split + [tail], axis=1)


def place_bias_kernel(key_ok_ref, got_ref, out_ref, *, rows, cols):
    main = cols // lanes
    half_lanes = lanes // 2
    low = lax.broadcasted_iota(jnp.int32, (1, lanes), 1) < half_lanes
    for n in range(0, got_ref.shape[0], 2):
        for h in range(got_ref.shape[1]):
            blocks = []
            even = [got_ref[n, h, b * rows : (b + 1) * rows] for b in range(main)]
            odd = [got_ref[n + 1, h, b * rows : (b + 1) * rows] for b in range(main)]
            even_tail = got_ref[n, h, main * rows :]
            odd_tail = got_ref[n + 1, h, main * rows :]
            even_last = jnp.concatenate(
                [even_tail, pltpu.roll(even_tail, half_lanes, 1)], axis=0
            )
            odd_last = jnp.concatenate([pltpu.roll(odd_tail, half_lanes, 1), odd_tail], axis=0)
            turned = [pltpu.roll(piece, half_lanes, 1) for piece in odd]
            blocks = list(even)
            before = even_last
            for piece in turned:
                blocks.append(jnp.where(low, before, piece))
                before = piece
            blocks.append(jnp.where(low, before, odd_last))
            for at, block in enumerate(blocks):
                lane = n * cols + at * lanes
                allowed = key_ok_ref[:, lane : lane + lanes] > 0
                out_ref[h, :, lane : lane + lanes] = jnp.where(allowed, block * log2e, far_below)


def place_bias(key_ok, gathered, wide_count, rows, cols):
    narrow_count = gathered.shape[0] // wide_count
    head_count = gathered.shape[1]
    length = wide_count * rows
    return pl.pallas_call(
        functools.partial(place_bias_kernel, rows=rows, cols=cols),
        out_shape=jax.ShapeDtypeStruct((head_count, length, length), jnp.float32),
        grid=(wide_count,),
        in_specs=[
            once((1, length)),
            pl.BlockSpec((narrow_count,) + gathered.shape[1:], lambda i: (i, 0, 0, 0)),
        ],
        out_specs=pl.BlockSpec((head_count, rows, length), lambda i: (0, i, 0)),
        compiler_params=params(16),
        cost_estimate=pl.CostEstimate(
            flops=gathered.size, bytes_accessed=8 * gathered.size, transcendentals=0
        ),
        name="place_bias",
    )(key_ok[None, :], gathered)


def turn_bias_kernel(key_ok_ref, got_ref, out_ref):
    queries = got_ref.shape[-1]
    plane = got_ref[:, 0, 0].reshape(-1, queries)
    allowed = key_ok_ref[...] > 0
    out_ref[0] = masked_bias(plane.T, allowed)


def turn_bias(key_ok, gathered, part):
    devices, _, head_count, rows, queries = gathered.shape
    length = devices * rows
    return pl.pallas_call(
        turn_bias_kernel,
        out_shape=jax.ShapeDtypeStruct((head_count, queries, length), jnp.float32),
        grid=(head_count,),
        in_specs=[
            once((1, length)),
            pl.BlockSpec((devices, 1, 1, rows, queries), lambda h: (0, part, h, 0, 0)),
        ],
        out_specs=pl.BlockSpec((1, queries, length), lambda h: (h, 0, 0)),
        compiler_params=params(),
        cost_estimate=pl.CostEstimate(
            flops=gathered.size, bytes_accessed=8 * gathered.size, transcendentals=0
        ),
        name="turn_bias",
    )(key_ok[None, :], gathered)


def lines_per_step(count, most):
    return max(per for per in range(1, most + 1) if count % per == 0)


def project_kernel(x_ref, w_ref, *rest, head_count, head_dim, normalise, strided):
    (*rest, scratch) = rest if strided else (*rest, None)
    sum_ref, (out_ref, norm_ref) = rest[0], ((rest[-1], None) if normalise else rest[-2:])
    width = head_count * head_dim
    pair = 2 * width
    channels = x_ref.shape[-1]
    per = out_ref.shape[0]
    if strided:
        stride = x_ref.shape[1]

        @pl.when(pl.program_id(0) == 0)
        def _():
            scratch[...] = x_ref[...].astype(jnp.float32).reshape(scratch.shape)

    for i in range(per):
        if strided:
            at = pl.program_id(0) * per + i
            normed = scratch[pl.ds(at, x_ref.shape[0], stride=stride), :].astype(jnp.bfloat16)
        elif normalise:
            normed = layer_norm(x_ref[:, i].reshape(-1, channels).astype(jnp.float32))
        else:
            normed = x_ref[i]
        projected = jnp.dot(normed, w_ref[...], preferred_element_type=jnp.float32).astype(
            jnp.bfloat16
        )
        first = pair + width
        queries = projected[:, first : first + pair].astype(jnp.float32)
        queries = queries * (head_dim ** (-0.5) * log2e)
        upper = queries.astype(jnp.bfloat16)
        lower = (queries - upper.astype(jnp.float32)).astype(jnp.bfloat16)
        spot = lax.broadcasted_iota(jnp.int32, (1, pair), 1)
        queries = jnp.where(spot % (2 * head_dim) < head_dim, upper, lower)
        measured = () if normalise else (queries, projected[:, :pair])
        for spot, part in enumerate(measured):
            squares = part.astype(jnp.float32)
            squares = (squares * squares).astype(jnp.bfloat16)
            sums = jnp.dot(squares, sum_ref[...], preferred_element_type=jnp.float32)
            norm_ref[i, spot : spot + 1, :] = jnp.max(sums, axis=0, keepdims=True)
        for block in range(projected.shape[1] // lanes):
            at = block * lanes
            if first <= at < first + pair:
                out_ref[i, block] = queries[:, at - first : at - first + lanes]
            else:
                out_ref[i, block] = projected[:, at : at + lanes]


def project(lines, packed, head_count, head_dim, kind, before=None, first=0, total=None):
    channels = lines.shape[-1]
    scratch = []
    if kind == "rows":
        pieces, count, cols = lines.shape[:3]
        length = pieces * cols
        per = lines_per_step(count, 2)
        spec = pl.BlockSpec((pieces, per, cols, channels), lambda i: (0, i, 0, 0))
    elif kind == "columns":
        length, count = lines.shape[:2]
        per = 1
        spec = once(lines.shape)
        scratch = [pltpu.VMEM((length * count, channels), jnp.float32)]
    else:
        count, length = lines.shape[:2]
        per = 1
        spec = pl.BlockSpec((1, length, channels), lambda i: (i, 0, 0))
    outs = packed.shape[1]
    total = count if total is None else total
    pair = 2 * head_count * head_dim
    owner = jnp.arange(pair)[:, None] // (2 * head_dim)
    sums = (owner == jnp.arange(lanes)[None, :]).astype(jnp.bfloat16)
    in_specs = [spec, once(packed.shape), once(sums.shape)]
    operands, aliases = [lines, packed, sums], {}
    if before is not None:
        in_specs.append(pl.BlockSpec(memory_space=pl.ANY))
        operands.append(before)
        aliases = {3: 0}
    skip = first // per
    measured = kind != "rows"
    got = pl.pallas_call(
        functools.partial(
            project_kernel,
            head_count=head_count,
            head_dim=head_dim,
            normalise=kind == "rows",
            strided=kind == "columns",
        ),
        out_shape=[
            jax.ShapeDtypeStruct((total, outs // lanes, length, lanes), jnp.bfloat16),
            jax.ShapeDtypeStruct((count, 8, lanes), jnp.float32),
        ][: 1 + measured],
        grid=(count // per,),
        in_specs=in_specs,
        out_specs=[
            pl.BlockSpec((per, outs // lanes, length, lanes), lambda i: (i + skip, 0, 0, 0)),
            pl.BlockSpec((per, 8, lanes), lambda i: (i, 0, 0)),
        ][: 1 + measured],
        scratch_shapes=scratch,
        input_output_aliases=aliases,
        compiler_params=params(),
        cost_estimate=pl.CostEstimate(
            flops=2 * lines.size * outs,
            bytes_accessed=2 * lines.size * (1 + outs // channels),
            transcendentals=0,
        ),
    )(*operands)
    if not measured:
        return got[0]
    out, norms = got
    most = jnp.max(norms[:, 0, :head_count] * norms[:, 1, :head_count], axis=-1) / 2
    return out, (most * 1.1 < safe_product**2).astype(jnp.int32)


def attend_lines(query_ref, key_ref, bias_refs, oks, bounded, head_count, head_dim):
    width = head_count * head_dim
    pair_blocks = 2 * width // lanes
    length = key_ref.shape[2]
    local = lax.broadcasted_iota(jnp.int32, (1, lanes), 1) // (2 * head_dim)
    owner = lax.broadcasted_iota(jnp.int32, (1, width), 1) // head_dim
    block_heads = lanes // (2 * head_dim)
    nothing = jnp.zeros((), jnp.bfloat16)

    def together(ref, i, first, *rest):
        parts = [ref[(i, first + n) + rest] for n in range(width // lanes)]
        parts = [part.reshape(-1, lanes) for part in parts]
        return parts[0] if len(parts) == 1 else jnp.concatenate(parts, axis=1)

    def score(i, at, h):
        block = h // block_heads
        queries = query_ref[i, block, :, at].reshape(-1, lanes)
        return lax.dot_general(
            jnp.where(local == h % block_heads, queries, nothing),
            key_ref[i, block],
            (((1,), (1,)), ((), ())),
            preferred_element_type=jnp.float32,
        )

    def head_sums(i, at, h, scores):
        scores = scores + bias_refs[at][h].reshape(-1, length)
        if not bounded:
            scores = scores - jnp.max(scores, axis=-1, keepdims=True)
        weights = jnp.exp2(scores).astype(jnp.bfloat16)
        values = together(key_ref, i, pair_blocks)
        values_ones = jnp.concatenate([values, jnp.ones_like(values)], axis=1)
        both_sums = jnp.dot(weights, values_ones, preferred_element_type=jnp.float32)
        return both_sums[:, :width] / both_sums[:, width:]

    def finish(i, at, summed):
        even = jnp.full((), 1.0 / length, jnp.float32).astype(jnp.bfloat16)
        values = together(key_ref, i, pair_blocks)
        total = jnp.sum(values.astype(jnp.float32), axis=0, keepdims=True)
        final = jnp.where(oks[i], summed, total * even.astype(jnp.float32))
        gates = together(query_ref, i, pair_blocks, slice(None), at).astype(jnp.float32)
        return (jax.nn.sigmoid(gates) * final).astype(jnp.bfloat16)

    spots = [(i, at) for i in range(key_ref.shape[0]) for at in range(len(bias_refs))]
    gated = {}
    if bounded is False:
        queries = query_ref.shape[2] * query_ref.shape[4]
        for i, at in spots:

            def one_head(h, summed):
                return jnp.where(owner == h, head_sums(i, at, h, score(i, at, h)), summed)

            start = jnp.zeros((queries, width), jnp.float32)
            gated[i, at] = finish(i, at, lax.fori_loop(0, head_count, one_head, start))
        return gated

    jobs = [(i, at, h) for i, at in spots for h in range(head_count)]
    coming = score(*jobs[0])
    summed = None
    for n, (i, at, h) in enumerate(jobs):
        scores = coming
        if n + 1 < len(jobs):
            coming = score(*jobs[n + 1])
        ratio = head_sums(i, at, h, scores)
        summed = ratio if h == 0 else jnp.where(owner == h, ratio, summed)
        if h == head_count - 1:
            gated[i, at] = finish(i, at, summed)
    return gated


def either_way(bounded_ref, lines, run):
    bounded = functools.reduce(jnp.minimum, [bounded_ref[line] for line in lines]) > 0
    pl.when(bounded)(lambda: run(True))
    pl.when(jnp.logical_not(bounded))(lambda: run(False))


def out_of(gated, w_out_ref):
    return jnp.dot(gated, w_out_ref[...], preferred_element_type=jnp.float32).astype(jnp.bfloat16)


def attend_rows_kernel(
    row_ok_ref, query_ref, key_ref, bias_ref, w_out_ref, x_ref, w_bias_ref, *rest, **sizes
):
    upd_ref, next_ref, nbias_ref = rest[-3:]
    per = key_ref.shape[0]
    lines = [pl.program_id(0) * per + i for i in range(per)]
    oks = [row_ok_ref[line] > 0 for line in lines]
    gated = attend_lines(query_ref, key_ref, [bias_ref], oks, None, **sizes)
    for i in range(per):
        update = out_of(gated[i, 0], w_out_ref)
        upd_ref[:, i] = update.reshape(upd_ref.shape[0], *upd_ref.shape[2:])
        features = x_ref[:, i].reshape(-1, x_ref.shape[-1]).astype(jnp.float32)
        normed = layer_norm(features + update.astype(jnp.float32))
        got = lax.dot_general(
            w_bias_ref[...], normed, (((1,), (1,)), ((), ())), preferred_element_type=jnp.float32
        )
        for h in range(nbias_ref.shape[0]):
            nbias_ref[h, pl.ds(lines[i], 1), :] = got[h : h + 1]
        if len(next_ref.shape) == 4:
            devices, _, cols, channels = next_ref.shape
            narrow_count = upd_ref.shape[0]
            spread = normed.astype(jnp.float32).reshape(
                narrow_count, devices // narrow_count, cols, channels
            )
            spread = spread.transpose(1, 0, 2, 3).reshape(devices, cols, channels)
            next_ref[:, i] = spread.astype(jnp.bfloat16)
        else:
            next_ref[i] = normed


def line_specs(projected, plan, per, first, parts, skip):
    blocks, chunks, piece = plan[:3]
    total, lane_blocks, length, _ = projected.shape
    half = lane_blocks // 2
    cut = projected.reshape(total, lane_blocks, blocks, chunks, piece, lanes)
    at = first // parts
    specs = [
        pl.BlockSpec(
            (per, half, blocks, parts, piece, lanes), lambda i, *_: (i + skip, 1, 0, at, 0, 0)
        ),
        pl.BlockSpec((per, half, length, lanes), lambda i, *_: (i + skip, 0, 0, 0)),
    ]
    return specs, [cut, projected]


def attend_rows(row_ok, projected, lines, bias, w_out, w_bias_rows, chunk, before, plan):
    blocks, chunks, piece, own, wide_count = plan
    pieces, count, cols, channels = lines.shape
    length = pieces * cols
    head_count = bias.shape[0]
    width = w_out.shape[0]
    head_dim = width // head_count
    direct = own % 8 == 0
    inner = blocks // pieces
    x_cut = lines.reshape(pieces, count, inner, chunks, piece, channels)
    bias_cut = bias.reshape(head_count, blocks, chunks, piece, length)
    per = lines_per_step(count, 2)
    queries = blocks * piece
    line_block = pl.BlockSpec(
        (pieces, per, inner, None, piece, channels), lambda i, ok: (0, i, 0, chunk, 0, 0)
    )
    if direct:
        next_shape = (wide_count * pieces, count, own, channels)
        next_spec = pl.BlockSpec(
            (wide_count * pieces, per, own, channels), lambda i, ok: (0, i, 0, 0)
        )
    else:
        next_shape = (count, queries, channels)
        next_spec = pl.BlockSpec((per, queries, channels), lambda i, ok: (i, 0, 0))
    nbias_shape = (head_count, count, queries)
    scores = count * head_count * length * queries
    in_specs, operands = line_specs(projected, plan, per, chunk, 1, 0)
    in_specs += [
        pl.BlockSpec(
            (head_count, blocks, None, piece, length),
            lambda i, ok: (0, 0, chunk, 0, 0),
            pipeline_mode=pl.Buffered(1),
        ),
        once(w_out.shape),
        line_block,
        once(w_bias_rows.shape),
    ]
    operands += [bias_cut, w_out, x_cut, w_bias_rows]
    aliases = {}
    if before is not None:
        in_specs.append(pl.BlockSpec(memory_space=pl.ANY))
        operands.append(before)
        aliases = {len(operands): 0}
    upd, nxt, nbias = pl.pallas_call(
        functools.partial(attend_rows_kernel, head_count=head_count, head_dim=head_dim),
        out_shape=[
            jax.ShapeDtypeStruct(x_cut.shape, jnp.bfloat16),
            jax.ShapeDtypeStruct(next_shape, jnp.bfloat16),
            jax.ShapeDtypeStruct(nbias_shape, jnp.float32),
        ],
        grid_spec=pltpu.PrefetchScalarGridSpec(
            num_scalar_prefetch=1,
            grid=(count // per,),
            in_specs=in_specs,
            out_specs=[line_block, next_spec, pl.BlockSpec(nbias_shape, lambda i, ok: (0, 0, 0))],
        ),
        input_output_aliases=aliases,
        compiler_params=params(),
        cost_estimate=pl.CostEstimate(
            flops=4 * scores * 128, bytes_accessed=8 * lines.size, transcendentals=scores
        ),
        name="attend_rows",
    )(row_ok, *operands)
    if not direct:
        nxt = nxt.reshape(count, pieces, wide_count, own, channels).transpose(2, 1, 0, 3, 4)
        nxt = nxt.reshape(wide_count * pieces, count, own, channels)
    return upd, nxt, nbias


def attend_columns_kernel(col_ok_ref, bounded_ref, query_ref, key_ref, *rest, parts, **sizes):
    bias_refs, w_out_ref, out_ref = rest[:parts], rest[parts], rest[parts + 1]
    scratch = rest[parts + 2 :]
    per = key_ref.shape[0]
    blocks, piece = query_ref.shape[2], query_ref.shape[4]
    lines = [pl.program_id(0) * per + i for i in range(per)]
    oks = [col_ok_ref[line] > 0 for line in lines]

    def run(bounded):
        gated = attend_lines(query_ref, key_ref, bias_refs, oks, bounded, **sizes)
        for i in range(per):
            for at in range(parts):
                update = out_of(gated[i, at], w_out_ref)
                if not scratch:
                    out_ref[:, i] = update.reshape(blocks, piece, update.shape[1])
                    continue
                stride = out_ref.shape[2]
                for m in range(blocks):
                    first = (m * parts + at) * piece * stride + lines[i]
                    scratch[0][pl.ds(first, piece, stride=stride), :] = update[
                        m * piece : (m + 1) * piece
                    ].astype(jnp.float32)

    either_way(bounded_ref, lines, run)
    if scratch:

        @pl.when(pl.program_id(0) == pl.num_programs(0) - 1)
        def _():
            out_ref[...] = scratch[0][...].reshape(out_ref.shape).astype(jnp.bfloat16)


def attend_columns(col_ok, bounded, projected, biases, w_out, first, skip, plan):
    blocks, _, piece, own, _ = plan
    length = projected.shape[2]
    count = col_ok.shape[0]
    parts = len(biases)
    head_count = biases[0].shape[0]
    width = w_out.shape[0]
    head_dim = width // head_count
    scores = count * head_count * length * blocks * parts * piece
    per = lines_per_step(count, 2) if parts == 1 and count > own else 1
    if own % 8 == 0:
        out_shape = (blocks, parts * piece, count, width)
        out_spec = pl.BlockSpec(out_shape, lambda i, *_: (0, 0, 0, 0))
        scratch = [pltpu.VMEM((blocks * parts * piece * count, width), jnp.float32)]
    else:
        out_shape = (blocks, count, parts * piece, width)
        out_spec = pl.BlockSpec((blocks, per, parts * piece, width), lambda i, *_: (0, i, 0, 0))
        scratch = []
    in_specs, operands = line_specs(projected, plan, per, first, parts, skip // per)
    return pl.pallas_call(
        functools.partial(
            attend_columns_kernel, parts=parts, head_count=head_count, head_dim=head_dim
        ),
        out_shape=jax.ShapeDtypeStruct(out_shape, jnp.bfloat16),
        grid_spec=pltpu.PrefetchScalarGridSpec(
            num_scalar_prefetch=2,
            grid=(count // per,),
            in_specs=in_specs + [once(biases[0].shape)] * parts + [once(w_out.shape)],
            out_specs=out_spec,
            scratch_shapes=scratch,
        ),
        compiler_params=params(),
        cost_estimate=pl.CostEstimate(
            flops=4 * scores * 128, bytes_accessed=8 * count * length * width, transcendentals=scores
        ),
        name="attend_columns",
    )(col_ok, bounded, *operands, *biases, w_out)


def settle_kernel(*refs, places, plan):
    _, chunks, piece, own, wide_count = plan
    tile_rows = chunks * piece
    out_ref = refs[-1]
    for j, (which, step) in enumerate(places):
        first = step * own
        for w in range(wide_count):
            inner, within = divmod(w * own, piece)
            col = inner * tile_rows + j * piece + within
            out_ref[:, col : col + own, :] = refs[which][w, :, first : first + own, :]


def settle(parts, first_row, before, places, plan, shape):
    wide_count, rows = parts[0].shape[:2]
    block = 16
    skip = first_row // block
    in_specs = [
        pl.BlockSpec((wide_count, block) + part.shape[2:], lambda i: (0, i, 0, 0))
        for part in parts
    ]
    operands, aliases = list(parts), {}
    if before is not None:
        in_specs.append(pl.BlockSpec(memory_space=pl.ANY))
        operands.append(before)
        aliases = {len(parts): 0}
    return pl.pallas_call(
        functools.partial(settle_kernel, places=places, plan=plan),
        out_shape=jax.ShapeDtypeStruct(shape, jnp.bfloat16),
        grid=(rows // block,),
        in_specs=in_specs,
        out_specs=pl.BlockSpec((block,) + shape[1:], lambda i: (i + skip, 0, 0)),
        input_output_aliases=aliases,
        compiler_params=params(),
        cost_estimate=pl.CostEstimate(
            flops=0, bytes_accessed=4 * parts[0].size * len(parts), transcendentals=0
        ),
        name="settle",
    )(*operands)


def bias_rows_of(w_bias):
    turned = w_bias.T
    return jnp.pad(turned, ((0, 16 - turned.shape[0]), (0, 0)))


def on_device(
    pair_act,
    residue_mask,
    w_proj_start,
    w_bias_start,
    w_out_start,
    w_proj_end,
    w_bias_end,
    w_out_end,
):
    wide_count = lax.axis_size("wide")
    narrow_count = lax.axis_size("narrow")
    wide_at = lax.axis_index("wide")
    narrow_at = lax.axis_index("narrow")
    tile_rows, tile_cols, channels = pair_act.shape
    head_count = w_bias_start.shape[1]
    head_dim = w_out_start.shape[0] // head_count
    length = wide_count * tile_rows
    row_count = tile_rows // narrow_count
    chunks = 1
    if tile_cols % tile_rows == 0:
        for tried in (3, 2):
            if tile_rows % (16 * tried) == 0 and tile_cols % (8 * tried * wide_count) == 0:
                chunks = tried
                break
    piece = tile_rows // chunks
    own = tile_cols // chunks // wide_count
    plan = (wide_count, chunks, piece, own, wide_count)
    key_ok = (residue_mask > 0).astype(jnp.int32)

    part = tile_bias(pair_act, bias_rows_of(w_bias_start), head_count)
    dense = tile_cols % lanes == lanes // 2 and tile_rows % 16 == 0 and narrow_count % 2 == 0
    if dense:
        part = pack_tile_bias(part)
    gathered = lax.all_gather(part, both_axes, axis=0, tiled=False)
    tile_in, part = lax.optimization_barrier((pair_act, part))
    lines = lax.all_to_all(
        tile_in.reshape(narrow_count, row_count, tile_cols, channels),
        "narrow",
        split_axis=0,
        concat_axis=0,
        tiled=True,
    )
    packed_start = pack_projection(w_proj_start, head_count, head_dim)
    projected = project(lines, packed_start, head_count, head_dim, "rows")
    if dense:
        bias = place_bias(key_ok, gathered, wide_count, tile_rows, tile_cols)
    else:
        bias = gathered.reshape(wide_count, narrow_count, head_count, tile_rows, tile_cols)
        bias = bias.transpose(2, 0, 3, 1, 4).reshape(head_count, length, length)
        bias = masked_bias(bias, key_ok > 0)

    row_ok = lax.dynamic_slice_in_dim(
        key_ok, wide_at * tile_rows + narrow_at * row_count, row_count
    )
    w_bias_rows = bias_rows_of(w_bias_end)
    order = [chunks - 1] + list(range(chunks - 1))
    columns, waiting, next_biases = {}, [], {}
    upd = None
    for step, j in enumerate(order):
        upd, nxt, nbias = attend_rows(
            row_ok, projected, lines, bias, w_out_start, w_bias_rows, j, upd, plan
        )
        waiting.append((j, nbias))
        if step in (0, chunks - 1):
            got = lax.all_gather(
                jnp.stack([nbias for _, nbias in waiting]), both_axes, axis=0, tiled=False
            )
            for n, (k, _) in enumerate(waiting):
                if row_count % 8 == 0:
                    turned = turn_bias(key_ok, got, n)
                else:
                    turned = got[:, n].transpose(1, 3, 0, 2).reshape(head_count, -1, length)
                    turned = masked_bias(turned, key_ok > 0)
                next_biases[k] = turned
            waiting = []
        got = lax.all_to_all(nxt, both_axes, split_axis=0, concat_axis=0, tiled=True)
        columns[j] = got.reshape(length, own, channels)
    mine = upd.reshape(narrow_count, row_count, tile_cols, channels)
    leaving = [
        lax.dynamic_index_in_dim(mine, (narrow_at + k) % narrow_count, 0)
        for k in range(1, narrow_count)
    ]
    leaving, mine = lax.optimization_barrier((leaving, mine))
    arrived = []
    for k in range(1, narrow_count):
        ring = [(n, (n + k) % narrow_count) for n in range(narrow_count)]
        arrived.append(lax.ppermute(leaving[k - 1], "narrow", ring))
    update_start = mine
    for k, got in enumerate(arrived, 1):
        source = (narrow_at + narrow_count - k) % narrow_count
        update_start = lax.dynamic_update_slice_in_dim(update_start, got, source, 0)
    update_start = update_start.reshape(tile_rows, tile_cols, channels)

    packed_end = pack_projection(w_proj_end, head_count, head_dim)
    soon = max(chunks - 1, 1)
    home_of = [(0, step) if step < soon else (soon, step - soon) for step in range(chunks)]
    projected_end, col_ok, bounded_end = {}, [], []
    for step, j in enumerate(order):
        group, place = home_of[step]
        lines_end = columns[j]
        if own % 8:
            lines_end = lines_end.transpose(1, 0, 2)
        projected_end[group], bounded = project(
            lines_end,
            packed_end,
            head_count,
            head_dim,
            "plain" if own % 8 else "columns",
            projected_end.get(group),
            place * own,
            (soon if group == 0 else chunks - soon) * own,
        )
        at = wide_at * own + jnp.arange(own)
        at = narrow_at * tile_cols + at // piece * tile_rows + j * piece + at % piece
        col_ok.append(key_ok[at])
        bounded_end.append(bounded)

    def columns_of(step, count, chosen):
        return attend_columns(
            jnp.concatenate(col_ok[step : step + count]),
            jnp.concatenate(bounded_end[step : step + count]),
            projected_end[home_of[step][0]],
            [next_biases[k] for k in chosen],
            w_out_end,
            chosen[0],
            home_of[step][1] * own,
            plan,
        )

    early = []
    for step, count in ((0, soon), (soon, chunks - soon)):
        if count:
            got = columns_of(step, count, order[:1])
            got = lax.all_to_all(got, "wide", split_axis=0, concat_axis=0, tiled=True)
            early.append(got)
    if chunks == 1:
        got = early[0]
        if own % 8:
            got = got.transpose(0, 2, 1, 3)
        return (update_start, got.transpose(1, 0, 2, 3).reshape(pair_act.shape))
    places = [(home_of[order.index(j)]) for j in range(chunks)]
    places = [(0 if group == 0 else 1, place) for group, place in places]
    settled = settle(early, (chunks - 1) * piece, None, places, plan, pair_act.shape)
    late = []
    for step in range(chunks):
        got = columns_of(step, 1, list(range(chunks - 1)))
        late.append(lax.all_to_all(got, "wide", split_axis=0, concat_axis=0, tiled=True))
    places = [(order.index(j), 0) for j in range(chunks)]
    return (update_start, settle(late, 0, settled, places, plan, pair_act.shape))


def solution(mesh):
    in_specs = (P("wide", "narrow", None), P(), P(), P(), P(), P(), P(), P())
    out_specs = (P("wide", "narrow", None), P("wide", "narrow", None))
    return jax.shard_map(
        on_device, mesh=mesh, in_specs=in_specs, out_specs=out_specs, check_vma=False
    )
```

```python
import functools

import jax
import jax.numpy as jnp
from jax import lax
from jax.experimental import pallas as pl
from jax.experimental.pallas import tpu as pltpu
from jax.sharding import PartitionSpec as P


norm_eps = 1e-05
log2e = 1.4426950408889634
far_below = -1e30
safe_product = 50.0
lanes = 128
both_axes = ("wide", "narrow")


def params(megabytes=60):
    return pltpu.CompilerParams(
        dimension_semantics=("arbitrary",), vmem_limit_bytes=megabytes * 1024 * 1024
    )


def once(shape):
    return pl.BlockSpec(
        shape, lambda *_: (0,) * len(shape), pipeline_mode=pl.Buffered(1)
    )


def layer_norm(features):
    average = jnp.mean(features, axis=-1, keepdims=True)
    centred = features - average
    spread = jnp.mean(centred * centred, axis=-1, keepdims=True)
    return (centred * lax.rsqrt(spread + norm_eps)).astype(jnp.bfloat16)


def masked_bias(bias, allowed):
    bias = jnp.where(allowed, bias * log2e, far_below)
    return bias - jnp.max(bias, axis=-1, keepdims=True)


def pack_projection(w_proj, head_count, head_dim):
    split = w_proj.reshape(w_proj.shape[0], head_count, 4, head_dim)
    twice = jnp.concatenate([split, split], axis=-1)
    parts = [twice[:, :, 1], split[:, :, 2], twice[:, :, 0], split[:, :, 3]]
    return jnp.concatenate([part.reshape(w_proj.shape[0], -1) for part in parts], axis=1)


def tile_bias_kernel(x_ref, w_ref, out_ref, *, head_count):
    for i in range(x_ref.shape[0]):
        normed = layer_norm(x_ref[i].astype(jnp.float32))
        got = lax.dot_general(
            w_ref[...], normed, (((1,), (1,)), ((), ())), preferred_element_type=jnp.float32
        )
        for h in range(head_count):
            out_ref[h, i : i + 1, :] = got[h : h + 1]


def tile_bias(tile, w_bias_rows, head_count):
    rows, cols, channels = tile.shape
    block = 8 if rows % 8 == 0 else rows
    return pl.pallas_call(
        functools.partial(tile_bias_kernel, head_count=head_count),
        out_shape=jax.ShapeDtypeStruct((head_count, rows, cols), jnp.float32),
        grid=(rows // block,),
        in_specs=[
            pl.BlockSpec((block, cols, channels), lambda i: (i, 0, 0)),
            once(w_bias_rows.shape),
        ],
        out_specs=pl.BlockSpec((head_count, block, cols), lambda i: (0, i, 0)),
        compiler_params=params(16),
        cost_estimate=pl.CostEstimate(
            flops=32 * tile.size, bytes_accessed=2 * tile.size, transcendentals=0
        ),
        name="tile_bias",
    )(tile, w_bias_rows)


def pack_tile_bias(part):
    rows, cols = part.shape[1:]
    main = cols // lanes * lanes
    left, right = part[:, :, :main], part[:, :, main:]
    half = rows // 2
    tail = jnp.concatenate([right[:, :half], right[:, half:]], axis=2)
    split = [left[:, :, at : at + lanes] for at in range(0, main, lanes)]
    return jnp.concatenate(split + [tail], axis=1)


def place_bias_kernel(key_ok_ref, got_ref, out_ref, *, rows, cols):
    main = cols // lanes
    half_lanes = lanes // 2
    low = lax.broadcasted_iota(jnp.int32, (1, lanes), 1) < half_lanes
    for n in range(0, got_ref.shape[0], 2):
        for h in range(got_ref.shape[1]):
            blocks = []
            even = [got_ref[n, h, b * rows : (b + 1) * rows] for b in range(main)]
            odd = [got_ref[n + 1, h, b * rows : (b + 1) * rows] for b in range(main)]
            even_tail = got_ref[n, h, main * rows :]
            odd_tail = got_ref[n + 1, h, main * rows :]
            even_last = jnp.concatenate(
                [even_tail, pltpu.roll(even_tail, half_lanes, 1)], axis=0
            )
            odd_last = jnp.concatenate([pltpu.roll(odd_tail, half_lanes, 1), odd_tail], axis=0)
            turned = [pltpu.roll(piece, half_lanes, 1) for piece in odd]
            blocks = list(even)
            before = even_last
            for piece in turned:
                blocks.append(jnp.where(low, before, piece))
                before = piece
            blocks.append(jnp.where(low, before, odd_last))
            for at, block in enumerate(blocks):
                lane = n * cols + at * lanes
                allowed = key_ok_ref[:, lane : lane + lanes] > 0
                out_ref[h, :, lane : lane + lanes] = jnp.where(allowed, block * log2e, far_below)


def place_bias(key_ok, gathered, wide_count, rows, cols):
    narrow_count = gathered.shape[0] // wide_count
    head_count = gathered.shape[1]
    length = wide_count * rows
    return pl.pallas_call(
        functools.partial(place_bias_kernel, rows=rows, cols=cols),
        out_shape=jax.ShapeDtypeStruct((head_count, length, length), jnp.float32),
        grid=(wide_count,),
        in_specs=[
            once((1, length)),
            pl.BlockSpec((narrow_count,) + gathered.shape[1:], lambda i: (i, 0, 0, 0)),
        ],
        out_specs=pl.BlockSpec((head_count, rows, length), lambda i: (0, i, 0)),
        compiler_params=params(16),
        cost_estimate=pl.CostEstimate(
            flops=gathered.size, bytes_accessed=8 * gathered.size, transcendentals=0
        ),
        name="place_bias",
    )(key_ok[None, :], gathered)


def turn_bias_kernel(key_ok_ref, got_ref, out_ref):
    queries = got_ref.shape[-1]
    plane = got_ref[:, 0, 0].reshape(-1, queries)
    allowed = key_ok_ref[...] > 0
    out_ref[0] = masked_bias(plane.T, allowed)


def turn_bias(key_ok, gathered, part):
    devices, _, head_count, rows, queries = gathered.shape
    length = devices * rows
    return pl.pallas_call(
        turn_bias_kernel,
        out_shape=jax.ShapeDtypeStruct((head_count, queries, length), jnp.float32),
        grid=(head_count,),
        in_specs=[
            once((1, length)),
            pl.BlockSpec((devices, 1, 1, rows, queries), lambda h: (0, part, h, 0, 0)),
        ],
        out_specs=pl.BlockSpec((1, queries, length), lambda h: (h, 0, 0)),
        compiler_params=params(),
        cost_estimate=pl.CostEstimate(
            flops=gathered.size, bytes_accessed=8 * gathered.size, transcendentals=0
        ),
        name="turn_bias",
    )(key_ok[None, :], gathered)


def lines_per_step(count, most):
    return max(per for per in range(1, most + 1) if count % per == 0)


def project_kernel(x_ref, w_ref, *rest, head_count, head_dim, normalise, strided):
    (*rest, scratch) = rest if strided else (*rest, None)
    sum_ref, (out_ref, norm_ref) = rest[0], ((rest[-1], None) if normalise else rest[-2:])
    width = head_count * head_dim
    pair = 2 * width
    channels = x_ref.shape[-1]
    per = out_ref.shape[0]
    if strided:
        stride = x_ref.shape[1]

        @pl.when(pl.program_id(0) == 0)
        def _():
            scratch[...] = x_ref[...].astype(jnp.float32).reshape(scratch.shape)

    for i in range(per):
        if strided:
            at = pl.program_id(0) * per + i
            normed = scratch[pl.ds(at, x_ref.shape[0], stride=stride), :].astype(jnp.bfloat16)
        elif normalise:
            normed = layer_norm(x_ref[:, i].reshape(-1, channels).astype(jnp.float32))
        else:
            normed = x_ref[i]
        projected = jnp.dot(normed, w_ref[...], preferred_element_type=jnp.float32).astype(
            jnp.bfloat16
        )
        first = pair + width
        queries = projected[:, first : first + pair].astype(jnp.float32)
        queries = queries * (head_dim ** (-0.5) * log2e)
        upper = queries.astype(jnp.bfloat16)
        lower = (queries - upper.astype(jnp.float32)).astype(jnp.bfloat16)
        spot = lax.broadcasted_iota(jnp.int32, (1, pair), 1)
        queries = jnp.where(spot % (2 * head_dim) < head_dim, upper, lower)
        measured = () if normalise else (queries, projected[:, :pair])
        for spot, part in enumerate(measured):
            squares = part.astype(jnp.float32)
            squares = (squares * squares).astype(jnp.bfloat16)
            sums = jnp.dot(squares, sum_ref[...], preferred_element_type=jnp.float32)
            norm_ref[i, spot : spot + 1, :] = jnp.max(sums, axis=0, keepdims=True)
        for block in range(projected.shape[1] // lanes):
            at = block * lanes
            if first <= at < first + pair:
                out_ref[i, block] = queries[:, at - first : at - first + lanes]
            else:
                out_ref[i, block] = projected[:, at : at + lanes]


def project(lines, packed, head_count, head_dim, kind, before=None, first=0, total=None):
    channels = lines.shape[-1]
    scratch = []
    if kind == "rows":
        pieces, count, cols = lines.shape[:3]
        length = pieces * cols
        per = lines_per_step(count, 2)
        spec = pl.BlockSpec((pieces, per, cols, channels), lambda i: (0, i, 0, 0))
    elif kind == "columns":
        length, count = lines.shape[:2]
        per = 1
        spec = once(lines.shape)
        scratch = [pltpu.VMEM((length * count, channels), jnp.float32)]
    else:
        count, length = lines.shape[:2]
        per = 1
        spec = pl.BlockSpec((1, length, channels), lambda i: (i, 0, 0))
    outs = packed.shape[1]
    total = count if total is None else total
    pair = 2 * head_count * head_dim
    owner = jnp.arange(pair)[:, None] // (2 * head_dim)
    sums = (owner == jnp.arange(lanes)[None, :]).astype(jnp.bfloat16)
    in_specs = [spec, once(packed.shape), once(sums.shape)]
    operands, aliases = [lines, packed, sums], {}
    if before is not None:
        in_specs.append(pl.BlockSpec(memory_space=pl.ANY))
        operands.append(before)
        aliases = {3: 0}
    skip = first // per
    measured = kind != "rows"
    got = pl.pallas_call(
        functools.partial(
            project_kernel,
            head_count=head_count,
            head_dim=head_dim,
            normalise=kind == "rows",
            strided=kind == "columns",
        ),
        out_shape=[
            jax.ShapeDtypeStruct((total, outs // lanes, length, lanes), jnp.bfloat16),
            jax.ShapeDtypeStruct((count, 8, lanes), jnp.float32),
        ][: 1 + measured],
        grid=(count // per,),
        in_specs=in_specs,
        out_specs=[
            pl.BlockSpec((per, outs // lanes, length, lanes), lambda i: (i + skip, 0, 0, 0)),
            pl.BlockSpec((per, 8, lanes), lambda i: (i, 0, 0)),
        ][: 1 + measured],
        scratch_shapes=scratch,
        input_output_aliases=aliases,
        compiler_params=params(),
        cost_estimate=pl.CostEstimate(
            flops=2 * lines.size * outs,
            bytes_accessed=2 * lines.size * (1 + outs // channels),
            transcendentals=0,
        ),
    )(*operands)
    if not measured:
        return got[0]
    out, norms = got
    most = jnp.max(norms[:, 0, :head_count] * norms[:, 1, :head_count], axis=-1) / 2
    return out, (most * 1.1 < safe_product**2).astype(jnp.int32)


def attend_lines(query_ref, key_ref, bias_refs, oks, bounded, head_count, head_dim):
    width = head_count * head_dim
    pair_blocks = 2 * width // lanes
    length = key_ref.shape[2]
    local = lax.broadcasted_iota(jnp.int32, (1, lanes), 1) // (2 * head_dim)
    owner = lax.broadcasted_iota(jnp.int32, (1, width), 1) // head_dim
    block_heads = lanes // (2 * head_dim)
    nothing = jnp.zeros((), jnp.bfloat16)

    def together(ref, i, first, *rest):
        parts = [ref[(i, first + n) + rest] for n in range(width // lanes)]
        parts = [part.reshape(-1, lanes) for part in parts]
        return parts[0] if len(parts) == 1 else jnp.concatenate(parts, axis=1)

    def score(i, at, h):
        block = h // block_heads
        queries = query_ref[i, block, :, at].reshape(-1, lanes)
        return lax.dot_general(
            jnp.where(local == h % block_heads, queries, nothing),
            key_ref[i, block],
            (((1,), (1,)), ((), ())),
            preferred_element_type=jnp.float32,
        )

    def head_sums(i, at, h, scores):
        scores = scores + bias_refs[at][h].reshape(-1, length)
        if not bounded:
            scores = scores - jnp.max(scores, axis=-1, keepdims=True)
        weights = jnp.exp2(scores).astype(jnp.bfloat16)
        values = together(key_ref, i, pair_blocks)
        values_ones = jnp.concatenate([values, jnp.ones_like(values)], axis=1)
        both_sums = jnp.dot(weights, values_ones, preferred_element_type=jnp.float32)
        return both_sums[:, :width] / both_sums[:, width:]

    def finish(i, at, summed):
        even = jnp.full((), 1.0 / length, jnp.float32).astype(jnp.bfloat16)
        values = together(key_ref, i, pair_blocks)
        total = jnp.sum(values.astype(jnp.float32), axis=0, keepdims=True)
        final = jnp.where(oks[i], summed, total * even.astype(jnp.float32))
        gates = together(query_ref, i, pair_blocks, slice(None), at).astype(jnp.float32)
        return (jax.nn.sigmoid(gates) * final).astype(jnp.bfloat16)

    spots = [(i, at) for i in range(key_ref.shape[0]) for at in range(len(bias_refs))]
    gated = {}
    if bounded is False:
        queries = query_ref.shape[2] * query_ref.shape[4]
        for i, at in spots:

            def one_head(h, summed):
                return jnp.where(owner == h, head_sums(i, at, h, score(i, at, h)), summed)

            start = jnp.zeros((queries, width), jnp.float32)
            gated[i, at] = finish(i, at, lax.fori_loop(0, head_count, one_head, start))
        return gated

    jobs = [(i, at, h) for i, at in spots for h in range(head_count)]
    coming = score(*jobs[0])
    summed = None
    for n, (i, at, h) in enumerate(jobs):
        scores = coming
        if n + 1 < len(jobs):
            coming = score(*jobs[n + 1])
        ratio = head_sums(i, at, h, scores)
        summed = ratio if h == 0 else jnp.where(owner == h, ratio, summed)
        if h == head_count - 1:
            gated[i, at] = finish(i, at, summed)
    return gated


def either_way(bounded_ref, lines, run):
    bounded = functools.reduce(jnp.minimum, [bounded_ref[line] for line in lines]) > 0
    pl.when(bounded)(lambda: run(True))
    pl.when(jnp.logical_not(bounded))(lambda: run(False))


def out_of(gated, w_out_ref):
    return jnp.dot(gated, w_out_ref[...], preferred_element_type=jnp.float32).astype(jnp.bfloat16)


def attend_rows_kernel(
    row_ok_ref, query_ref, key_ref, bias_ref, w_out_ref, x_ref, w_bias_ref, *rest, **sizes
):
    upd_ref, next_ref, nbias_ref = rest[-3:]
    per = key_ref.shape[0]
    lines = [pl.program_id(0) * per + i for i in range(per)]
    oks = [row_ok_ref[line] > 0 for line in lines]
    gated = attend_lines(query_ref, key_ref, [bias_ref], oks, None, **sizes)
    for i in range(per):
        update = out_of(gated[i, 0], w_out_ref)
        upd_ref[:, i] = update.reshape(upd_ref.shape[0], *upd_ref.shape[2:])
        features = x_ref[:, i].reshape(-1, x_ref.shape[-1]).astype(jnp.float32)
        normed = layer_norm(features + update.astype(jnp.float32))
        got = lax.dot_general(
            w_bias_ref[...], normed, (((1,), (1,)), ((), ())), preferred_element_type=jnp.float32
        )
        for h in range(nbias_ref.shape[0]):
            nbias_ref[h, pl.ds(lines[i], 1), :] = got[h : h + 1]
        if len(next_ref.shape) == 4:
            devices, _, cols, channels = next_ref.shape
            narrow_count = upd_ref.shape[0]
            spread = normed.astype(jnp.float32).reshape(
                narrow_count, devices // narrow_count, cols, channels
            )
            spread = spread.transpose(1, 0, 2, 3).reshape(devices, cols, channels)
            next_ref[:, i] = spread.astype(jnp.bfloat16)
        else:
            next_ref[i] = normed


def line_specs(projected, plan, per, first, parts, skip):
    blocks, chunks, piece = plan[:3]
    total, lane_blocks, length, _ = projected.shape
    half = lane_blocks // 2
    cut = projected.reshape(total, lane_blocks, blocks, chunks, piece, lanes)
    at = first // parts
    specs = [
        pl.BlockSpec(
            (per, half, blocks, parts, piece, lanes), lambda i, *_: (i + skip, 1, 0, at, 0, 0)
        ),
        pl.BlockSpec((per, half, length, lanes), lambda i, *_: (i + skip, 0, 0, 0)),
    ]
    return specs, [cut, projected]


def attend_rows(row_ok, projected, lines, bias, w_out, w_bias_rows, chunk, before, plan):
    blocks, chunks, piece, own, wide_count = plan
    pieces, count, cols, channels = lines.shape
    length = pieces * cols
    head_count = bias.shape[0]
    width = w_out.shape[0]
    head_dim = width // head_count
    direct = own % 8 == 0
    inner = blocks // pieces
    x_cut = lines.reshape(pieces, count, inner, chunks, piece, channels)
    bias_cut = bias.reshape(head_count, blocks, chunks, piece, length)
    per = lines_per_step(count, 2)
    queries = blocks * piece
    line_block = pl.BlockSpec(
        (pieces, per, inner, None, piece, channels), lambda i, ok: (0, i, 0, chunk, 0, 0)
    )
    if direct:
        next_shape = (wide_count * pieces, count, own, channels)
        next_spec = pl.BlockSpec(
            (wide_count * pieces, per, own, channels), lambda i, ok: (0, i, 0, 0)
        )
    else:
        next_shape = (count, queries, channels)
        next_spec = pl.BlockSpec((per, queries, channels), lambda i, ok: (i, 0, 0))
    nbias_shape = (head_count, count, queries)
    scores = count * head_count * length * queries
    in_specs, operands = line_specs(projected, plan, per, chunk, 1, 0)
    in_specs += [
        pl.BlockSpec(
            (head_count, blocks, None, piece, length),
            lambda i, ok: (0, 0, chunk, 0, 0),
            pipeline_mode=pl.Buffered(1),
        ),
        once(w_out.shape),
        line_block,
        once(w_bias_rows.shape),
    ]
    operands += [bias_cut, w_out, x_cut, w_bias_rows]
    aliases = {}
    if before is not None:
        in_specs.append(pl.BlockSpec(memory_space=pl.ANY))
        operands.append(before)
        aliases = {len(operands): 0}
    upd, nxt, nbias = pl.pallas_call(
        functools.partial(attend_rows_kernel, head_count=head_count, head_dim=head_dim),
        out_shape=[
            jax.ShapeDtypeStruct(x_cut.shape, jnp.bfloat16),
            jax.ShapeDtypeStruct(next_shape, jnp.bfloat16),
            jax.ShapeDtypeStruct(nbias_shape, jnp.float32),
        ],
        grid_spec=pltpu.PrefetchScalarGridSpec(
            num_scalar_prefetch=1,
            grid=(count // per,),
            in_specs=in_specs,
            out_specs=[line_block, next_spec, pl.BlockSpec(nbias_shape, lambda i, ok: (0, 0, 0))],
        ),
        input_output_aliases=aliases,
        compiler_params=params(),
        cost_estimate=pl.CostEstimate(
            flops=4 * scores * 128, bytes_accessed=8 * lines.size, transcendentals=scores
        ),
        name="attend_rows",
    )(row_ok, *operands)
    if not direct:
        nxt = nxt.reshape(count, pieces, wide_count, own, channels).transpose(2, 1, 0, 3, 4)
        nxt = nxt.reshape(wide_count * pieces, count, own, channels)
    return upd, nxt, nbias


def attend_columns_kernel(col_ok_ref, bounded_ref, query_ref, key_ref, *rest, parts, **sizes):
    bias_refs, w_out_ref, out_ref = rest[:parts], rest[parts], rest[parts + 1]
    scratch = rest[parts + 2 :]
    per = key_ref.shape[0]
    blocks, piece = query_ref.shape[2], query_ref.shape[4]
    lines = [pl.program_id(0) * per + i for i in range(per)]
    oks = [col_ok_ref[line] > 0 for line in lines]

    def run(bounded):
        gated = attend_lines(query_ref, key_ref, bias_refs, oks, bounded, **sizes)
        for i in range(per):
            for at in range(parts):
                update = out_of(gated[i, at], w_out_ref)
                if not scratch:
                    out_ref[:, i] = update.reshape(blocks, piece, update.shape[1])
                    continue
                stride = out_ref.shape[2]
                for m in range(blocks):
                    first = (m * parts + at) * piece * stride + lines[i]
                    scratch[0][pl.ds(first, piece, stride=stride), :] = update[
                        m * piece : (m + 1) * piece
                    ].astype(jnp.float32)

    either_way(bounded_ref, lines, run)
    if scratch:

        @pl.when(pl.program_id(0) == pl.num_programs(0) - 1)
        def _():
            out_ref[...] = scratch[0][...].reshape(out_ref.shape).astype(jnp.bfloat16)


def attend_columns(col_ok, bounded, projected, biases, w_out, first, skip, plan):
    blocks, _, piece, own, _ = plan
    length = projected.shape[2]
    count = col_ok.shape[0]
    parts = len(biases)
    head_count = biases[0].shape[0]
    width = w_out.shape[0]
    head_dim = width // head_count
    scores = count * head_count * length * blocks * parts * piece
    per = lines_per_step(count, 2) if parts == 1 and count > own else 1
    if own % 8 == 0:
        out_shape = (blocks, parts * piece, count, width)
        out_spec = pl.BlockSpec(out_shape, lambda i, *_: (0, 0, 0, 0))
        scratch = [pltpu.VMEM((blocks * parts * piece * count, width), jnp.float32)]
    else:
        out_shape = (blocks, count, parts * piece, width)
        out_spec = pl.BlockSpec((blocks, per, parts * piece, width), lambda i, *_: (0, i, 0, 0))
        scratch = []
    in_specs, operands = line_specs(projected, plan, per, first, parts, skip // per)
    return pl.pallas_call(
        functools.partial(
            attend_columns_kernel, parts=parts, head_count=head_count, head_dim=head_dim
        ),
        out_shape=jax.ShapeDtypeStruct(out_shape, jnp.bfloat16),
        grid_spec=pltpu.PrefetchScalarGridSpec(
            num_scalar_prefetch=2,
            grid=(count // per,),
            in_specs=in_specs + [once(biases[0].shape)] * parts + [once(w_out.shape)],
            out_specs=out_spec,
            scratch_shapes=scratch,
        ),
        compiler_params=params(),
        cost_estimate=pl.CostEstimate(
            flops=4 * scores * 128, bytes_accessed=8 * count * length * width, transcendentals=scores
        ),
        name="attend_columns",
    )(col_ok, bounded, *operands, *biases, w_out)


def settle_kernel(*refs, places, plan):
    _, chunks, piece, own, wide_count = plan
    tile_rows = chunks * piece
    out_ref = refs[-1]
    for j, (which, step) in enumerate(places):
        first = step * own
        for w in range(wide_count):
            inner, within = divmod(w * own, piece)
            col = inner * tile_rows + j * piece + within
            out_ref[:, col : col + own, :] = refs[which][w, :, first : first + own, :]


def settle(parts, first_row, before, places, plan, shape):
    wide_count, rows = parts[0].shape[:2]
    block = 16
    skip = first_row // block
    in_specs = [
        pl.BlockSpec((wide_count, block) + part.shape[2:], lambda i: (0, i, 0, 0))
        for part in parts
    ]
    operands, aliases = list(parts), {}
    if before is not None:
        in_specs.append(pl.BlockSpec(memory_space=pl.ANY))
        operands.append(before)
        aliases = {len(parts): 0}
    return pl.pallas_call(
        functools.partial(settle_kernel, places=places, plan=plan),
        out_shape=jax.ShapeDtypeStruct(shape, jnp.bfloat16),
        grid=(rows // block,),
        in_specs=in_specs,
        out_specs=pl.BlockSpec((block,) + shape[1:], lambda i: (i + skip, 0, 0)),
        input_output_aliases=aliases,
        compiler_params=params(),
        cost_estimate=pl.CostEstimate(
            flops=0, bytes_accessed=4 * parts[0].size * len(parts), transcendentals=0
        ),
        name="settle",
    )(*operands)


def bias_rows_of(w_bias):
    turned = w_bias.T
    return jnp.pad(turned, ((0, 16 - turned.shape[0]), (0, 0)))


def on_device(
    pair_act,
    residue_mask,
    w_proj_start,
    w_bias_start,
    w_out_start,
    w_proj_end,
    w_bias_end,
    w_out_end,
):
    wide_count = lax.axis_size("wide")
    narrow_count = lax.axis_size("narrow")
    wide_at = lax.axis_index("wide")
    narrow_at = lax.axis_index("narrow")
    tile_rows, tile_cols, channels = pair_act.shape
    head_count = w_bias_start.shape[1]
    head_dim = w_out_start.shape[0] // head_count
    length = wide_count * tile_rows
    row_count = tile_rows // narrow_count
    chunks = 1
    if tile_cols % tile_rows == 0:
        for tried in (3, 2):
            if tile_rows % (16 * tried) == 0 and tile_cols % (8 * tried * wide_count) == 0:
                chunks = tried
                break
    piece = tile_rows // chunks
    own = tile_cols // chunks // wide_count
    plan = (wide_count, chunks, piece, own, wide_count)
    key_ok = (residue_mask > 0).astype(jnp.int32)

    part = tile_bias(pair_act, bias_rows_of(w_bias_start), head_count)
    dense = tile_cols % lanes == lanes // 2 and tile_rows % 16 == 0 and narrow_count % 2 == 0
    if dense:
        part = pack_tile_bias(part)
    gathered = lax.all_gather(part, both_axes, axis=0, tiled=False)
    tile_in, part = lax.optimization_barrier((pair_act, part))
    lines = lax.all_to_all(
        tile_in.reshape(narrow_count, row_count, tile_cols, channels),
        "narrow",
        split_axis=0,
        concat_axis=0,
        tiled=True,
    )
    packed_start = pack_projection(w_proj_start, head_count, head_dim)
    projected = project(lines, packed_start, head_count, head_dim, "rows")
    if dense:
        bias = place_bias(key_ok, gathered, wide_count, tile_rows, tile_cols)
    else:
        bias = gathered.reshape(wide_count, narrow_count, head_count, tile_rows, tile_cols)
        bias = bias.transpose(2, 0, 3, 1, 4).reshape(head_count, length, length)
        bias = masked_bias(bias, key_ok > 0)

    row_ok = lax.dynamic_slice_in_dim(
        key_ok, wide_at * tile_rows + narrow_at * row_count, row_count
    )
    w_bias_rows = bias_rows_of(w_bias_end)
    order = [chunks - 1] + list(range(chunks - 1))
    columns, waiting, next_biases = {}, [], {}
    upd = None
    for step, j in enumerate(order):
        upd, nxt, nbias = attend_rows(
            row_ok, projected, lines, bias, w_out_start, w_bias_rows, j, upd, plan
        )
        waiting.append((j, nbias))
        if step in (0, chunks - 1):
            got = lax.all_gather(
                jnp.stack([nbias for _, nbias in waiting]), both_axes, axis=0, tiled=False
            )
            for n, (k, _) in enumerate(waiting):
                if row_count % 8 == 0:
                    turned = turn_bias(key_ok, got, n)
                else:
                    turned = got[:, n].transpose(1, 3, 0, 2).reshape(head_count, -1, length)
                    turned = masked_bias(turned, key_ok > 0)
                next_biases[k] = turned
            waiting = []
        got = lax.all_to_all(nxt, both_axes, split_axis=0, concat_axis=0, tiled=True)
        columns[j] = got.reshape(length, own, channels)
    mine = upd.reshape(narrow_count, row_count, tile_cols, channels)
    leaving = [
        lax.dynamic_index_in_dim(mine, (narrow_at + k) % narrow_count, 0)
        for k in range(1, narrow_count)
    ]
    leaving, mine = lax.optimization_barrier((leaving, mine))
    arrived = []
    for k in range(1, narrow_count):
        ring = [(n, (n + k) % narrow_count) for n in range(narrow_count)]
        arrived.append(lax.ppermute(leaving[k - 1], "narrow", ring))
    update_start = mine
    for k, got in enumerate(arrived, 1):
        source = (narrow_at + narrow_count - k) % narrow_count
        update_start = lax.dynamic_update_slice_in_dim(update_start, got, source, 0)
    update_start = update_start.reshape(tile_rows, tile_cols, channels)

    packed_end = pack_projection(w_proj_end, head_count, head_dim)
    soon = max(chunks - 1, 1)
    home_of = [(0, step) if step < soon else (soon, step - soon) for step in range(chunks)]
    projected_end, col_ok, bounded_end = {}, [], []
    for step, j in enumerate(order):
        group, place = home_of[step]
        lines_end = columns[j]
        if own % 8:
            lines_end = lines_end.transpose(1, 0, 2)
        projected_end[group], bounded = project(
            lines_end,
            packed_end,
            head_count,
            head_dim,
            "plain" if own % 8 else "columns",
            projected_end.get(group),
            place * own,
            (soon if group == 0 else chunks - soon) * own,
        )
        at = wide_at * own + jnp.arange(own)
        at = narrow_at * tile_cols + at // piece * tile_rows + j * piece + at % piece
        col_ok.append(key_ok[at])
        bounded_end.append(bounded)

    def columns_of(step, count, chosen):
        return attend_columns(
            jnp.concatenate(col_ok[step : step + count]),
            jnp.concatenate(bounded_end[step : step + count]),
            projected_end[home_of[step][0]],
            [next_biases[k] for k in chosen],
            w_out_end,
            chosen[0],
            home_of[step][1] * own,
            plan,
        )

    early = []
    for step, count in ((0, soon), (soon, chunks - soon)):
        if count:
            early.append(columns_of(step, count, order[:1]))
    got = early[0] if chunks == 1 else jnp.concatenate(early, axis=2)
    got = lax.all_to_all(got, "wide", split_axis=0, concat_axis=0, tiled=True)
    if chunks == 1:
        if own % 8:
            got = got.transpose(0, 2, 1, 3)
        return (update_start, got.transpose(1, 0, 2, 3).reshape(pair_act.shape))
    places = [(0, order.index(j)) for j in range(chunks)]
    settled = settle([got], (chunks - 1) * piece, None, places, plan, pair_act.shape)
    late = []
    for step in range(chunks):
        got = columns_of(step, 1, list(range(chunks - 1)))
        late.append(lax.all_to_all(got, "wide", split_axis=0, concat_axis=0, tiled=True))
    places = [(order.index(j), 0) for j in range(chunks)]
    return (update_start, settle(late, 0, settled, places, plan, pair_act.shape))


def solution(mesh):
    in_specs = (P("wide", "narrow", None), P(), P(), P(), P(), P(), P(), P())
    out_specs = (P("wide", "narrow", None), P("wide", "narrow", None))
    return jax.shard_map(
        on_device, mesh=mesh, in_specs=in_specs, out_specs=out_specs, check_vma=False
    )
```
